32 devices in a mesh: space: 16 (over z, y, core), band: 2 (over x).
Axes of the slice: x: 2, y: 2, z: 4, core: 2. Of those that a mesh axis runs over, the one named last changes fastest.
Arguments:
- orbitals: float32 [48, 16, 8, 16, 128], P('band', 'space'), may hold values from -100 to 100
- potential: float32 [16, 8, 16, 128], P('space'), may hold values from 0.5 to 4
Outputs:
- basis: float32 [48, 16, 8, 16, 128], P('band', 'space')
- factor: float32 [48, 48], replicated
The draws below stay inside these ranges and needn't reach their ends.
All inputs are finite; a program needn't handle non-finite values.
Results may differ from the reference program's by a relative error of at most 0.0003.
Values sent between devices are 32-bit elements; how exact they have to be, the bound alone decides.
A program may use at most 64 MiB of HBM per device.

```python
import math
import jax
import jax.numpy as jnp
from jax import lax

NORB = 48
DEG = 4
CX = 8
CY = 16
CZ = 128
TILES = 16
TX = 1


def draw_orbitals(key, part):
    shape = (NORB, TILES, CX, CY, CZ)
    field_shape = (1, TILES, CX, CY, CZ)
    key_base, key_cells, key_orbs, key_common, key_weights, key_spread = jax.random.split(key, 6)
    tile_position = jnp.arange(TILES, dtype=jnp.float32) / max(TILES - 1, 1)
    tile_scale = (3.0 ** tile_position).reshape(1, TILES, 1, 1, 1)
    cell_scale = 10.0 ** jax.random.uniform(key_cells, field_shape, jnp.float32)
    orbital_scale = 10.0 ** jax.random.uniform(key_orbs, (NORB, 1, 1, 1, 1), jnp.float32)
    weights = jax.random.uniform(key_weights, (NORB, 1, 1, 1, 1), jnp.float32, 0.6, 1.4)
    spread = jax.random.uniform(key_spread, (NORB, 1, 1, 1, 1), jnp.float32)
    spread = (spread - jnp.min(spread)) / (jnp.max(spread) - jnp.min(spread))
    lowest = 0.012
    own_weight = lowest ** (1.0 - spread)
    base = jnp.clip(jax.random.normal(key_base, shape, jnp.float32), -4.0, 4.0)
    common = jnp.clip(jax.random.normal(key_common, field_shape, jnp.float32), -4.0, 4.0)
    mixed = weights * common + own_weight * base
    return (0.025 * mixed * cell_scale * orbital_scale * tile_scale).astype(jnp.float32)


def block_scale(stream_key, shape, shards, smallest, largest):
    level = 1.0
    for axis_at, parts in shards:
        heights = jax.random.uniform(jax.random.fold_in(jax.random.fold_in(stream_key, 6), axis_at), (parts,), jnp.float32, smallest / len(shards), largest / len(shards))
        level = level * jnp.repeat(jnp.exp(heights), shape[axis_at] // parts).reshape((-1,) + (1,) * (len(shape) - 1 - axis_at))
    return level


def setup_inputs(seed: int = 0) -> dict:
    splits = jax.random.split(jax.random.key(seed), 3)
    return {
        "orbitals": draw_orbitals(jax.random.fold_in(splits[2], 71), 0),
        "potential": jnp.clip(jnp.exp(math.log(4.0) - 2.0794415 * jax.random.uniform(splits[1], (TILES, CX, CY, CZ), jnp.float32) ** block_scale(splits[1], (TILES, CX, CY, CZ), ((0, 16),), -0.2, 0.2)), 0.5, 4.0),
    }


coefficients = (-205.0 / 72.0, 8.0 / 5.0, -1.0 / 5.0, 8.0 / 315.0, -1.0 / 560.0)
centre_value = 9.25
half_range = 4.75
filter_scale = 1.0 / 32.0

def to_grid(tiles):
    shaped = tiles.reshape(TX, 4, 4, CX, CY, CZ)
    return shaped.transpose(0, 3, 1, 4, 2, 5).reshape(TX * CX, 4 * CY, 4 * CZ)

def from_grid(grid_values):
    shaped = grid_values.reshape(TX, CX, 4, CY, 4, CZ)
    return shaped.transpose(0, 2, 4, 1, 3, 5).reshape(TILES, CX, CY, CZ)

def laplacian(values):
    total = 3.0 * coefficients[0] * values
    for axis_dim in range(3):
        widths = [(0, 0), (0, 0), (0, 0)]
        widths[axis_dim] = (4, 4)
        padded = jnp.pad(values, widths)
        extent = values.shape[axis_dim]
        for offset in range(1, 5):
            upper = lax.slice_in_dim(padded, 4 + offset, 4 + offset + extent, axis=axis_dim)
            lower = lax.slice_in_dim(padded, 4 - offset, 4 - offset + extent, axis=axis_dim)
            total = total + coefficients[offset] * (upper + lower)
    return total

def reference(orbitals, potential):
    grid_potential = to_grid(potential)

    def hamiltonian(values):
        return -0.5 * laplacian(values) + grid_potential * values

    def filter_one(tiles):
        start_values = to_grid(tiles)
        previous = start_values
        current = (hamiltonian(start_values) - centre_value * start_values) / half_range
        for step_index in range(DEG - 1):
            following = 2.0 * (hamiltonian(current) - centre_value * current) / half_range - previous
            previous, current = (current, following)
        return from_grid(current * filter_scale)
    filtered = lax.map(filter_one, orbitals)
    flat = filtered.reshape(NORB, -1)
    total_cells = flat.shape[1]
    identity = jnp.eye(NORB, dtype=jnp.float32)
    current = flat
    lowers = []
    for round_index in range(2):
        gram = jnp.dot(current.astype(jnp.float32), current.T.astype(jnp.float32), precision=lax.Precision.HIGHEST, preferred_element_type=jnp.float32) / total_cells
        lower = jnp.linalg.cholesky(gram)
        inverse = jax.scipy.linalg.solve_triangular(lower, identity, lower=True)
        current = jnp.dot(inverse.astype(jnp.float32), current.astype(jnp.float32), precision=lax.Precision.HIGHEST, preferred_element_type=jnp.float32)
        lowers.append(lower)
    factor = jnp.dot(lowers[0].astype(jnp.float32), lowers[1].astype(jnp.float32), precision=lax.Precision.HIGHEST, preferred_element_type=jnp.float32).T
    return (current.reshape(orbitals.shape), factor)
```

```python
import functools

import jax
import jax.numpy as jnp
from jax import lax
from jax.experimental import pallas as pl
from jax.experimental.pallas import tpu as pltpu
from jax.sharding import PartitionSpec as P

DEG = 4
MESH = pl.DeviceIdType.MESH

coefficients = (-205.0 / 72.0, 8.0 / 5.0, -1.0 / 5.0, 8.0 / 315.0, -1.0 / 560.0)
centre_value = 9.25
half_range = 4.75
filter_scale = 1.0 / 32.0


def shifted(block, axis, distance):
    devices = range(lax.axis_size(axis))
    route = [(i - distance, i) for i in devices if i - distance in devices]
    return lax.ppermute(block, axis, route)


def padded_along(field_in, axis_dim, stride, tile_count, coordinate):
    extent = field_in.shape[axis_dim]
    if tile_count == 1:
        widths = [(0, 0)] * field_in.ndim
        widths[axis_dim] = (4, 4)
        return jnp.pad(field_in, widths)
    top_layers = lax.slice_in_dim(field_in, extent - 4, extent, axis=axis_dim)
    bottom_layers = lax.slice_in_dim(field_in, 0, 4, axis=axis_dim)
    received = []
    for direction, portion, retain in (
        (1, top_layers, coordinate > 0),
        (-1, bottom_layers, coordinate < tile_count - 1),
    ):
        arrived = shifted(portion, "space", direction * stride)
        received.append(jnp.where(retain, arrived, jnp.zeros_like(arrived)))
    return jnp.concatenate([received[0], field_in, received[1]], axis=axis_dim)


def hamiltonian(field_in, potential, layout):
    total = 3.0 * coefficients[0] * field_in
    for axis_dim, stride, tile_count, coordinate in layout:
        padded = padded_along(field_in, axis_dim, stride, tile_count, coordinate)
        extent = field_in.shape[axis_dim]
        for offset in range(1, 5):
            upper = lax.slice_in_dim(padded, 4 + offset, 4 + offset + extent, axis=axis_dim)
            lower = lax.slice_in_dim(padded, 4 - offset, 4 - offset + extent, axis=axis_dim)
            total = total + coefficients[offset] * (upper + lower)
    return -0.5 * total + potential * field_in


def orthonormalize(flat, reduce_gram, total_cells, rows, own_count):
    count_orbs = flat.shape[0]
    identity = jnp.eye(count_orbs, dtype=jnp.float32)
    current = flat
    lowers = []
    for round_index in range(2):
        partial_gram = jnp.tensordot(
            current, current, axes=(tuple(range(1, current.ndim)),) * 2,
            precision=lax.Precision.HIGHEST, preferred_element_type=jnp.float32,
        )
        gram = reduce_gram(partial_gram) / total_cells
        lower = jnp.linalg.cholesky(gram)
        inverse = jax.scipy.linalg.solve_triangular(lower, identity, lower=True)
        if round_index == 1:
            inverse = lax.dynamic_slice_in_dim(inverse, rows, own_count, axis=0)
        current = jnp.tensordot(
            inverse, current, axes=1, precision=lax.Precision.HIGHEST, preferred_element_type=jnp.float32
        )
        lowers.append(lower)
    factor = jnp.dot(
        lowers[0], lowers[1], precision=lax.Precision.HIGHEST, preferred_element_type=jnp.float32
    ).T
    return (current, factor)


def reduce_everywhere(partial_gram):
    total = partial_gram
    size = lax.axis_size("space")
    step = 1
    while step < size:
        route = [(i, i ^ step) for i in range(size)]
        total = total + lax.ppermute(total, "space", route)
        step *= 2
    return total


def general_shards(orbitals, potential):
    tile_index = lax.axis_index("space")
    layout = (
        (2, 16, lax.axis_size("space") // 16, tile_index // 16),
        (3, 4, 4, tile_index // 4 % 4),
        (4, 1, 4, tile_index % 4),
    )
    previous = orbitals
    current = (hamiltonian(orbitals, potential, layout) - centre_value * orbitals) / half_range
    for step_index in range(DEG - 1):
        following = (
            2.0 * (hamiltonian(current, potential, layout) - centre_value * current) / half_range
            - previous
        )
        previous, current = (current, following)
    filtered = current * filter_scale
    own_count = filtered.shape[0]
    everything = lax.all_gather(filtered, "band", axis=0, tiled=True)
    total_cells = everything[0].size * lax.axis_size("space")
    rows = lax.axis_index("band") * own_count
    ortho, factor = orthonormalize(everything, reduce_everywhere, total_cells, rows, own_count)
    return (ortho.reshape(filtered.shape), factor)


NY, NXM, NZ = 16, 4, 128
ROWS = 16
UP, DOWN, LEFT, RIGHT = 0, 1, 2, 3


def kernel(ng, x_ref, pot_ref, f_ref, y0, y1, y2, y3, pack, from_left, from_right, weight, send, recv, xsend, xrecv):
    ys = (y0, y1, y2, y3)
    t = lax.axis_index("space")
    band = lax.axis_index("band")
    ty, tz = t // 4, t % 4
    lane = lax.broadcasted_iota(jnp.int32, (8, NZ), 1)
    sub = lax.broadcasted_iota(jnp.int32, (8, NZ), 0)
    even = sub % 2 == 0
    zero = jnp.zeros((8, NZ), jnp.float32)
    seat = lane % 8

    sends = (ty > 0, ty < 3, tz > 0, tz < 3)
    gets = (ty < 3, ty > 0, tz < 3, tz > 0)
    offset = (-4, 4, -1, 1)

    def halo(d, s, g):
        if d == UP:
            src, dst = ys[s].at[g, pl.ds(4, 4)], ys[s].at[g, pl.ds(20, 4)]
        elif d == DOWN:
            src, dst = ys[s].at[g, pl.ds(16, 4)], ys[s].at[g, pl.ds(0, 4)]
        elif d == LEFT:
            src, dst = pack.at[s, g], from_right.at[s, g]
        else:
            src, dst = pack.at[s, g], from_left.at[s, g]
        return pltpu.make_async_remote_copy(
            src_ref=src, dst_ref=dst, send_sem=send.at[d, s, g], recv_sem=recv.at[d, s, g],
            device_id=(t + offset[d], band), device_id_type=MESH,
        )

    def exchange(g, half):
        part = f_ref.at[band * ng + g, pl.ds(8 * half, 8)]
        return pltpu.make_async_remote_copy(
            src_ref=part, dst_ref=part, send_sem=xsend.at[g, half], recv_sem=xrecv.at[g, half],
            device_id=(t, 1 - band), device_id_type=MESH,
        )

    def arrival(g, half):
        part = f_ref.at[(1 - band) * ng + g, pl.ds(8 * half, 8)]
        return pltpu.make_async_remote_copy(
            src_ref=part, dst_ref=part, send_sem=xsend.at[g, half], recv_sem=xrecv.at[g, half],
            device_id=(t, 1 - band), device_id_type=MESH,
        )

    def clear(step, _):
        for s in range(4):
            @pl.when(ty == 0)
            def _():
                ys[s][step, 0:4] = jnp.zeros((4, NXM, 8, NZ), jnp.float32)

            @pl.when(ty == 3)
            def _():
                ys[s][step, 20:24] = jnp.zeros((4, NXM, 8, NZ), jnp.float32)

            @pl.when(tz == 0)
            def _():
                from_left[s, step] = jnp.zeros((4, 8, NZ), jnp.float32)

            @pl.when(tz == 3)
            def _():
                from_right[s, step] = jnp.zeros((4, 8, NZ), jnp.float32)
        return 0

    barrier = pltpu.get_barrier_semaphore()
    for d in range(4):
        @pl.when(sends[d])
        def _():
            pl.semaphore_signal(barrier, inc=1, device_id=(t + offset[d], band), device_id_type=MESH)
    pl.semaphore_signal(barrier, inc=1, device_id=(t, 1 - band), device_id_type=MESH)
    lax.fori_loop(0, ng, clear, 0)

    def weigh(y, _):
        for xm in range(NXM):
            low = pot_ref[pl.ds(xm * NY + y, 1), :]
            high = pot_ref[pl.ds((4 + xm) * NY + y, 1), :]
            both = jnp.where(even, jnp.broadcast_to(low, (8, NZ)), jnp.broadcast_to(high, (8, NZ)))
            weight[y, xm] = (2.0 / half_range) * (both - (1.5 * coefficients[0] + centre_value))
        return 0

    lax.fori_loop(0, NY, weigh, 0)
    count = sum(jnp.int32(c) for c in sends) + 1
    pl.semaphore_wait(barrier, count)

    def start_halos(s, g):
        for d in range(4):
            @pl.when(sends[d])
            def _():
                halo(d, s, g).start()

    def prepare(g):
        def quad(q, _):
            packed = zero
            for j in range(ROWS):
                y, xm = 4 * q + j // 4, j % 4
                v = x_ref[pl.ds(g * 512 + xm * NY + y, 8, stride=64), :]
                y0[g, 4 + y, xm] = v
                packed = jnp.where(lane // 8 == j, pltpu.roll(v, 8 * j + 4, 1), packed)
            pack[0, g, q] = packed
            return 0

        lax.fori_loop(0, 4, quad, 0)
        start_halos(0, g)

    def unit(s, g):
        for d in range(4):
            @pl.when(gets[d])
            def _():
                halo(d, s, g).wait_recv()
        now = ys[s]
        scale = (1.0 if s == 0 else 2.0) / half_range * (filter_scale if s == 3 else 1.0)
        keep = filter_scale if s == 3 else 1.0
        ck = [None] + [-0.5 * scale * c for c in coefficients[1:]]

        def quad(q, _):
            diff = jnp.where(seat < 4, from_left[s, g, q], from_right[s, g, q]) - pack[s, g, q]
            fix = zero
            for k in range(1, 5):
                plus = jnp.where((seat >= 4) & (seat - k < 4), ck[k], 0.0)
                minus = jnp.where((seat < 4) & (seat + k >= 4), ck[k], 0.0)
                fix = fix + plus * pltpu.roll(diff, k, 1) + minus * pltpu.roll(diff, NZ - k, 1)
            packed = zero
            for yy in range(4):
                y = 4 * q + yy
                v = [now[g, 4 + y, xm] for xm in range(NXM)]
                upper = [jnp.where(even, pltpu.roll(a, 7, 0), 0.0) for a in v]
                lower = [jnp.where(even, 0.0, pltpu.roll(a, 1, 0)) for a in v]
                for xm in range(NXM):
                    j = 4 * yy + xm
                    acc = None
                    for k in range(1, 5):
                        total = pltpu.roll(v[xm], k, 1) + pltpu.roll(v[xm], NZ - k, 1)
                        total = total + (now[g, 4 + y - k, xm] + now[g, 4 + y + k, xm])
                        right = v[xm + k] if xm + k < 4 else upper[xm + k - 4]
                        left = v[xm - k] if xm >= k else lower[xm - k + 4]
                        total = total + (right + left)
                        acc = ck[k] * total if acc is None else acc + ck[k] * total
                    mine = pltpu.roll(fix, (NZ - 8 * j - 4) % NZ, 1)
                    acc = acc + jnp.where((lane < 4) | (lane >= NZ - 4), mine, 0.0)
                    w = weight[y, xm]
                    if s == 0:
                        new = acc + 0.5 * w * v[xm]
                    elif s == 3:
                        new = acc + (keep * w) * v[xm] - keep * ys[s - 1][g, 4 + y, xm]
                    else:
                        new = acc + w * v[xm] - ys[s - 1][g, 4 + y, xm]
                    if s < 3:
                        ys[s + 1][g, 4 + y, xm] = new
                        packed = jnp.where(lane // 8 == j, pltpu.roll(new, (8 * j + 4) % NZ, 1), packed)
                    else:
                        f_ref[band * ng + g, y, xm] = new
            if s < 3:
                pack[s + 1, g, q] = packed
            return 0

        lax.fori_loop(0, 4, quad, 0)
        if s < 3:
            start_halos(s + 1, g)
        else:
            exchange(g, 0).start()
            exchange(g, 1).start()

    lead = 2
    for g in range(lead):
        prepare(jnp.int32(g))

    def turn(step, _):
        for s in (3, 2, 1, 0):
            g = step - s
            @pl.when((g >= 0) & (g < ng))
            def _():
                unit(s, g)

        @pl.when(step + lead < ng)
        def _():
            prepare(step + lead)
        return 0

    lax.fori_loop(0, ng + 3, turn, 0)

    def finish(g, _):
        for half in range(2):
            arrival(g, half).wait_recv()
            exchange(g, half).wait_send()
        for s in range(4):
            for d in range(4):
                @pl.when(sends[d])
                def _():
                    halo(d, s, g).wait_send()
        return 0

    lax.fori_loop(0, ng, finish, 0)


def filter_all(orbitals, potential):
    own = orbitals.shape[0]
    ng = own // 4
    field = pltpu.VMEM((ng, NY + 8, NXM, 8, NZ), jnp.float32)
    edges = pltpu.VMEM((4, ng, 4, 8, NZ), jnp.float32)
    return pl.pallas_call(
        functools.partial(kernel, ng),
        out_shape=jax.ShapeDtypeStruct((2 * ng, NY, NXM, 8, NZ), jnp.float32),
        in_specs=[pl.BlockSpec(memory_space=pltpu.VMEM)] * 2,
        out_specs=pl.BlockSpec(memory_space=pltpu.VMEM),
        scratch_shapes=[
            field, field, field, field, edges, edges, edges,
            pltpu.VMEM((NY, NXM, 8, NZ), jnp.float32),
            pltpu.SemaphoreType.DMA((4, 4, ng)),
            pltpu.SemaphoreType.DMA((4, 4, ng)),
            pltpu.SemaphoreType.DMA((ng, 2)),
            pltpu.SemaphoreType.DMA((ng, 2)),
        ],
        compiler_params=pltpu.CompilerParams(
            collective_id=0, has_side_effects=True, vmem_limit_bytes=50 * 1024 * 1024
        ),
    )(orbitals.reshape(own * 128, NZ), potential.reshape(128, NZ))


def shards(orbitals, potential):
    own = orbitals.shape[0]
    everything = filter_all(orbitals, potential)
    flat = everything.reshape(2 * own // 4, NY, NXM, 4, 2, NZ).transpose(0, 3, 4, 2, 1, 5).reshape(2 * own, 8, NY, NZ)
    total_cells = flat[0].size * lax.axis_size("space")
    rows = lax.axis_index("band") * own
    ortho, factor = orthonormalize(flat, reduce_everywhere, total_cells, rows, own)
    return (ortho.reshape(orbitals.shape), factor)


def solution(mesh):
    covered = mesh.shape["space"] == 16 and mesh.shape["band"] == 2
    return jax.shard_map(
        shards if covered else general_shards,
        mesh=mesh,
        in_specs=(P("band", "space", None, None, None), P("space", None, None, None)),
        out_specs=(P("band", "space", None, None, None), P()),
        check_vma=False,
    )
```

```python
import functools

import jax
import jax.numpy as jnp
from jax import lax
from jax.experimental import pallas as pl
from jax.experimental.pallas import tpu as pltpu
from jax.sharding import PartitionSpec as P

DEG = 4
MESH = pl.DeviceIdType.MESH

coefficients = (-205.0 / 72.0, 8.0 / 5.0, -1.0 / 5.0, 8.0 / 315.0, -1.0 / 560.0)
centre_value = 9.25
half_range = 4.75
filter_scale = 1.0 / 32.0


def shifted(block, axis, distance):
    devices = range(lax.axis_size(axis))
    route = [(i - distance, i) for i in devices if i - distance in devices]
    return lax.ppermute(block, axis, route)


def padded_along(field_in, axis_dim, stride, tile_count, coordinate):
    extent = field_in.shape[axis_dim]
    if tile_count == 1:
        widths = [(0, 0)] * field_in.ndim
        widths[axis_dim] = (4, 4)
        return jnp.pad(field_in, widths)
    top_layers = lax.slice_in_dim(field_in, extent - 4, extent, axis=axis_dim)
    bottom_layers = lax.slice_in_dim(field_in, 0, 4, axis=axis_dim)
    received = []
    for direction, portion, retain in (
        (1, top_layers, coordinate > 0),
        (-1, bottom_layers, coordinate < tile_count - 1),
    ):
        arrived = shifted(portion, "space", direction * stride)
        received.append(jnp.where(retain, arrived, jnp.zeros_like(arrived)))
    return jnp.concatenate([received[0], field_in, received[1]], axis=axis_dim)


def hamiltonian(field_in, potential, layout):
    total = 3.0 * coefficients[0] * field_in
    for axis_dim, stride, tile_count, coordinate in layout:
        padded = padded_along(field_in, axis_dim, stride, tile_count, coordinate)
        extent = field_in.shape[axis_dim]
        for offset in range(1, 5):
            upper = lax.slice_in_dim(padded, 4 + offset, 4 + offset + extent, axis=axis_dim)
            lower = lax.slice_in_dim(padded, 4 - offset, 4 - offset + extent, axis=axis_dim)
            total = total + coefficients[offset] * (upper + lower)
    return -0.5 * total + potential * field_in


def orthonormalize(flat, reduce_gram, total_cells, rows, own_count):
    count_orbs = flat.shape[0]
    identity = jnp.eye(count_orbs, dtype=jnp.float32)
    current = flat
    lowers = []
    for round_index in range(2):
        partial_gram = jnp.tensordot(
            current, current, axes=(tuple(range(1, current.ndim)),) * 2,
            precision=lax.Precision.HIGHEST, preferred_element_type=jnp.float32,
        )
        gram = reduce_gram(partial_gram) / total_cells
        lower = jnp.linalg.cholesky(gram)
        inverse = jax.scipy.linalg.solve_triangular(lower, identity, lower=True)
        if round_index == 1:
            inverse = lax.dynamic_slice_in_dim(inverse, rows, own_count, axis=0)
        current = jnp.tensordot(
            inverse, current, axes=1, precision=lax.Precision.HIGHEST, preferred_element_type=jnp.float32
        )
        lowers.append(lower)
    factor = jnp.dot(
        lowers[0], lowers[1], precision=lax.Precision.HIGHEST, preferred_element_type=jnp.float32
    ).T
    return (current, factor)


def reduce_everywhere(partial_gram):
    total = partial_gram
    size = lax.axis_size("space")
    step = 1
    while step < size:
        route = [(i, i ^ step) for i in range(size)]
        total = total + lax.ppermute(total, "space", route)
        step *= 2
    return total


def general_shards(orbitals, potential):
    tile_index = lax.axis_index("space")
    layout = (
        (2, 16, lax.axis_size("space") // 16, tile_index // 16),
        (3, 4, 4, tile_index // 4 % 4),
        (4, 1, 4, tile_index % 4),
    )
    previous = orbitals
    current = (hamiltonian(orbitals, potential, layout) - centre_value * orbitals) / half_range
    for step_index in range(DEG - 1):
        following = (
            2.0 * (hamiltonian(current, potential, layout) - centre_value * current) / half_range
            - previous
        )
        previous, current = (current, following)
    filtered = current * filter_scale
    own_count = filtered.shape[0]
    everything = lax.all_gather(filtered, "band", axis=0, tiled=True)
    total_cells = everything[0].size * lax.axis_size("space")
    rows = lax.axis_index("band") * own_count
    ortho, factor = orthonormalize(everything, reduce_everywhere, total_cells, rows, own_count)
    return (ortho.reshape(filtered.shape), factor)


NY, NXM, NZ = 16, 4, 128
ROWS = 16
UP, DOWN, LEFT, RIGHT = 0, 1, 2, 3


def kernel(
    ng, x_ref, pot_ref, out_ref, factor_ref, f_ref, y0, y1, y2, y3, pack, from_left, from_right, weight,
    gram, spread, plane, column, send, recv, xsend, xrecv, psend, precv, csend, crecv,
):
    ys = (y0, y1, y2, y3)
    cells = 16 * 8 * NY * NZ
    t = lax.axis_index("space")
    band = lax.axis_index("band")
    ty, tz = t // 4, t % 4
    lane = lax.broadcasted_iota(jnp.int32, (8, NZ), 1)
    sub = lax.broadcasted_iota(jnp.int32, (8, NZ), 0)
    even = sub % 2 == 0
    zero = jnp.zeros((8, NZ), jnp.float32)
    seat = lane % 8

    sends = (ty > 0, ty < 3, tz > 0, tz < 3)
    gets = (ty < 3, ty > 0, tz < 3, tz > 0)
    offset = (-4, 4, -1, 1)

    def halo(d, s, g):
        if d == UP:
            src, dst = ys[s].at[g, pl.ds(4, 4)], ys[s].at[g, pl.ds(20, 4)]
        elif d == DOWN:
            src, dst = ys[s].at[g, pl.ds(16, 4)], ys[s].at[g, pl.ds(0, 4)]
        elif d == LEFT:
            src, dst = pack.at[s, g], from_right.at[s, g]
        else:
            src, dst = pack.at[s, g], from_left.at[s, g]
        return pltpu.make_async_remote_copy(
            src_ref=src, dst_ref=dst, send_sem=send.at[d, s, g], recv_sem=recv.at[d, s, g],
            device_id=(t + offset[d], band), device_id_type=MESH,
        )

    def exchange(g, half):
        part = f_ref.at[band * ng + g, pl.ds(8 * half, 8)]
        return pltpu.make_async_remote_copy(
            src_ref=part, dst_ref=part, send_sem=xsend.at[g, half], recv_sem=xrecv.at[g, half],
            device_id=(t, 1 - band), device_id_type=MESH,
        )

    def arrival(g, half):
        part = f_ref.at[(1 - band) * ng + g, pl.ds(8 * half, 8)]
        return pltpu.make_async_remote_copy(
            src_ref=part, dst_ref=part, send_sem=xsend.at[g, half], recv_sem=xrecv.at[g, half],
            device_id=(t, 1 - band), device_id_type=MESH,
        )

    def clear(step, _):
        for s in range(4):
            @pl.when(ty == 0)
            def _():
                ys[s][step, 0:4] = jnp.zeros((4, NXM, 8, NZ), jnp.float32)

            @pl.when(ty == 3)
            def _():
                ys[s][step, 20:24] = jnp.zeros((4, NXM, 8, NZ), jnp.float32)

            @pl.when(tz == 0)
            def _():
                from_left[s, step] = jnp.zeros((4, 8, NZ), jnp.float32)

            @pl.when(tz == 3)
            def _():
                from_right[s, step] = jnp.zeros((4, 8, NZ), jnp.float32)
        return 0

    seat_in_plane = band * 4 + tz

    def in_plane(step):
        other = (seat_in_plane + step) % 8
        return other, (4 * ty + other % 4, other // 4)

    def in_column(step):
        other = (ty + step) % 4
        return other, (4 * other + tz, band)

    barrier = pltpu.get_barrier_semaphore()
    for step in range(1, 8):
        pl.semaphore_signal(barrier, inc=1, device_id=in_plane(step)[1], device_id_type=MESH)
    for step in range(1, 4):
        pl.semaphore_signal(barrier, inc=1, device_id=in_column(step)[1], device_id_type=MESH)
    lax.fori_loop(0, ng, clear, 0)

    def weigh(y, _):
        for xm in range(NXM):
            low = pot_ref[pl.ds(xm * NY + y, 1), :]
            high = pot_ref[pl.ds((4 + xm) * NY + y, 1), :]
            both = jnp.where(even, jnp.broadcast_to(low, (8, NZ)), jnp.broadcast_to(high, (8, NZ)))
            weight[y, xm] = (2.0 / half_range) * (both - (1.5 * coefficients[0] + centre_value))
        return 0

    lax.fori_loop(0, NY, weigh, 0)
    pl.semaphore_wait(barrier, 10)

    def start_halos(s, g):
        for d in range(4):
            @pl.when(sends[d])
            def _():
                halo(d, s, g).start()

    def prepare(g):
        def quad(q, _):
            packed = zero
            for j in range(ROWS):
                y, xm = 4 * q + j // 4, j % 4
                v = x_ref[pl.ds(g * 512 + xm * NY + y, 8, stride=64), :]
                y0[g, 4 + y, xm] = v
                packed = jnp.where(lane // 8 == j, pltpu.roll(v, 8 * j + 4, 1), packed)
            pack[0, g, q] = packed
            return 0

        lax.fori_loop(0, 4, quad, 0)
        start_halos(0, g)

    def unit(s, g):
        for d in range(4):
            @pl.when(gets[d])
            def _():
                halo(d, s, g).wait_recv()
        now = ys[s]
        scale = (1.0 if s == 0 else 2.0) / half_range * (filter_scale if s == 3 else 1.0)
        keep = filter_scale if s == 3 else 1.0
        ck = [None] + [-0.5 * scale * c for c in coefficients[1:]]

        def quad(q, _):
            diff = jnp.where(seat < 4, from_left[s, g, q], from_right[s, g, q]) - pack[s, g, q]
            fix = zero
            for k in range(1, 5):
                plus = jnp.where((seat >= 4) & (seat - k < 4), ck[k], 0.0)
                minus = jnp.where((seat < 4) & (seat + k >= 4), ck[k], 0.0)
                fix = fix + plus * pltpu.roll(diff, k, 1) + minus * pltpu.roll(diff, NZ - k, 1)
            packed = zero
            for yy in range(4):
                y = 4 * q + yy
                v = [now[g, 4 + y, xm] for xm in range(NXM)]
                upper = [jnp.where(even, pltpu.roll(a, 7, 0), 0.0) for a in v]
                lower = [jnp.where(even, 0.0, pltpu.roll(a, 1, 0)) for a in v]
                for xm in range(NXM):
                    j = 4 * yy + xm
                    acc = None
                    for k in range(1, 5):
                        total = pltpu.roll(v[xm], k, 1) + pltpu.roll(v[xm], NZ - k, 1)
                        total = total + (now[g, 4 + y - k, xm] + now[g, 4 + y + k, xm])
                        right = v[xm + k] if xm + k < 4 else upper[xm + k - 4]
                        left = v[xm - k] if xm >= k else lower[xm - k + 4]
                        total = total + (right + left)
                        acc = ck[k] * total if acc is None else acc + ck[k] * total
                    mine = pltpu.roll(fix, (NZ - 8 * j - 4) % NZ, 1)
                    acc = acc + jnp.where((lane < 4) | (lane >= NZ - 4), mine, 0.0)
                    w = weight[y, xm]
                    if s == 0:
                        new = acc + 0.5 * w * v[xm]
                    elif s == 3:
                        new = acc + (keep * w) * v[xm] - keep * ys[s - 1][g, 4 + y, xm]
                    else:
                        new = acc + w * v[xm] - ys[s - 1][g, 4 + y, xm]
                    if s < 3:
                        ys[s + 1][g, 4 + y, xm] = new
                        packed = jnp.where(lane // 8 == j, pltpu.roll(new, (8 * j + 4) % NZ, 1), packed)
                    else:
                        f_ref[band * ng + g, y, xm] = new
            if s < 3:
                pack[s + 1, g, q] = packed
            return 0

        lax.fori_loop(0, 4, quad, 0)
        if s < 3:
            start_halos(s + 1, g)
        else:
            exchange(g, 1 - band).start()

            @pl.when((band == 0) & (g >= 1) & (g < ng - 1))
            def _():
                exchange(g - 1, 0).start()

    lead = 2
    for g in range(lead):
        prepare(jnp.int32(g))

    def turn(step, _):
        for s in (3, 2, 1, 0):
            g = step - s
            @pl.when((g >= 0) & (g < ng))
            def _():
                unit(s, g)

        @pl.when(step + lead < ng)
        def _():
            prepare(step + lead)
        return 0

    lax.fori_loop(0, ng + 3, turn, 0)

    def shares(g, _):
        arrival(g, band).wait_recv()
        return 0

    lax.fori_loop(0, ng, shares, 0)

    @pl.when(band == 0)
    def _():
        exchange(ng - 2, 0).start()
        exchange(ng - 1, 0).start()

    nr = 16 * ng
    norb = nr // 2
    tiles = norb // 8
    even_lane = lane % 2 == 0

    def block(y, xm):
        return f_ref[:, y, xm].reshape(nr, NZ)

    def pair(i):
        y, xm = 8 * band + i // 2, 2 * (i % 2)
        return jnp.concatenate([block(y, xm), block(y, xm + 1)], axis=1)

    def inner(a):
        return lax.dot_general(
            a, a, (((1,), (1,)), ((), ())), precision=lax.Precision.HIGHEST, preferred_element_type=jnp.float32
        )

    def reduce_all(which, partial):
        gram[...] = jnp.zeros((nr, NZ), jnp.float32)
        gram[:, 0:nr] = partial
        first_half = gram[pl.ds(0, norb, stride=2), :]
        second_half = gram[pl.ds(1, norb, stride=2), :]
        both = [
            (first_half[8 * i : 8 * i + 8] + pltpu.roll(second_half[8 * i : 8 * i + 8], NZ - 1, 1)) * (1.0 / cells)
            for i in range(tiles)
        ]
        for i in range(tiles // 2):
            packed = jnp.where(even_lane, both[i], pltpu.roll(both[i + tiles // 2], 1, 1))
            plane[which, seat_in_plane, pl.ds(8 * i, 8)] = packed

        def to_plane(step):
            other, device = in_plane(step)
            mine = plane.at[which, seat_in_plane]
            return other, pltpu.make_async_remote_copy(
                src_ref=mine, dst_ref=mine, send_sem=psend.at[which, step], recv_sem=precv.at[which, seat_in_plane],
                device_id=device, device_id_type=MESH,
            )

        def from_plane(step):
            other, device = in_plane(step)
            theirs = plane.at[which, other]
            return pltpu.make_async_remote_copy(
                src_ref=theirs, dst_ref=theirs, send_sem=psend.at[which, step], recv_sem=precv.at[which, other],
                device_id=device, device_id_type=MESH,
            )

        def to_column(step):
            other, device = in_column(step)
            mine = column.at[which, ty]
            return pltpu.make_async_remote_copy(
                src_ref=mine, dst_ref=mine, send_sem=csend.at[which, step], recv_sem=crecv.at[which, ty],
                device_id=device, device_id_type=MESH,
            )

        def from_column(step):
            other, device = in_column(step)
            theirs = column.at[which, other]
            return pltpu.make_async_remote_copy(
                src_ref=theirs, dst_ref=theirs, send_sem=csend.at[which, step], recv_sem=crecv.at[which, other],
                device_id=device, device_id_type=MESH,
            )

        for step in range(1, 8):
            to_plane(step)[1].start()
        for step in range(1, 8):
            from_plane(step).wait_recv()
        for i in range(tiles // 2):
            column[which, ty, pl.ds(8 * i, 8)] = sum(plane[which, o, pl.ds(8 * i, 8)] for o in range(8))
        for step in range(1, 4):
            to_column(step).start()
        for step in range(1, 4):
            from_column(step).wait_recv()
        full = [sum(column[which, o, pl.ds(8 * i, 8)] for o in range(4)) for i in range(tiles // 2)]
        for step in range(1, 8):
            to_plane(step)[1].wait_send()
        for step in range(1, 4):
            to_column(step).wait_send()
        return [jnp.where(even_lane, a, pltpu.roll(a, 1, 1)) for a in full] + [
            jnp.where(even_lane, pltpu.roll(a, NZ - 1, 1), a) for a in full
        ]

    def eliminate(a, b):
        a, b = list(a), list(b)
        pivots = [zero + 1.0 for _ in range(tiles)]
        for j in range(norb):
            at, r = j // 8, j % 8
            row = jnp.broadcast_to(a[at][r : r + 1, :], (8, NZ))
            row_b = jnp.broadcast_to(b[at][r : r + 1, :], (8, NZ))
            pivot = jnp.broadcast_to(row[:, 2 * j : 2 * j + 1], (8, NZ))
            pivots[at] = jnp.where(sub == r, pivot, pivots[at])
            inverse = 1.0 / pivot
            row = row * inverse
            row_b = row_b * inverse
            for i in range(at, tiles):
                col = jnp.broadcast_to(a[i][:, 2 * j : 2 * j + 1], (8, NZ))
                if i == at:
                    if r == 7:
                        continue
                    col = jnp.where(sub > r, col, 0.0)
                a[i] = a[i] - col * row
                b[i] = b[i] - col * row_b
        scale = [lax.rsqrt(p) for p in pivots]
        upper = [jnp.where(lane // 2 >= sub + 8 * i, a[i] * scale[i], 0.0) for i in range(tiles)]
        return upper, [b[i] * scale[i] for i in range(tiles)]

    def spread_rows(a):
        whole = jnp.concatenate(a, axis=0)
        is_even = jnp.concatenate([even_lane] * tiles, axis=0)
        spread[pl.ds(0, norb, stride=2), :] = jnp.where(is_even, whole, 0.0)
        spread[pl.ds(1, norb, stride=2), :] = jnp.where(is_even, 0.0, whole)

    def highest(a, b):
        return jnp.dot(a, b, precision=lax.Precision.HIGHEST, preferred_element_type=jnp.float32)

    def add_first(i, total):
        return total + inner(pair(i))

    gram1 = reduce_all(0, lax.fori_loop(0, 16, add_first, jnp.zeros((nr, nr), jnp.float32)))
    unit_rows = [jnp.where((lane // 2 == sub + 8 * i), 1.0, 0.0) for i in range(tiles)]
    upper1, inverse1 = eliminate(gram1, unit_rows)
    spread_rows(inverse1)

    def add_second(i, total):
        return total + inner(highest(spread[:, 0:nr], pair(i)))

    gram2 = reduce_all(1, lax.fori_loop(0, 16, add_second, jnp.zeros((nr, nr), jnp.float32)))
    upper2, inverse2 = eliminate(gram2, inverse1)
    spread_rows(inverse2)
    own = nr // 2

    @pl.when(band == 0)
    def _():
        def rows(i, _):
            y, xm = i // NXM, i % NXM
            out_ref[pl.ds(xm * NY + y, own, stride=64), :] = highest(
                spread[0:own, 0:own], f_ref[0:ng, y, xm].reshape(own, NZ)
            )
            return 0

        lax.fori_loop(0, NY * NXM, rows, 0)

    @pl.when(band == 1)
    def _():
        def late(g, _):
            arrival(g, 0).wait_recv()
            return 0

        lax.fori_loop(0, ng, late, 0)

        def rows(i, _):
            y, xm = i // NXM, i % NXM
            out_ref[pl.ds(xm * NY + y, own, stride=64), :] = highest(spread[own:nr, 0:nr], block(y, xm))
            return 0

        lax.fori_loop(0, NY * NXM, rows, 0)

    pick = jnp.where(
        lax.broadcasted_iota(jnp.int32, (NZ, norb), 0) == 2 * lax.broadcasted_iota(jnp.int32, (NZ, norb), 1), 1.0, 0.0
    )
    one = highest(jnp.concatenate(upper1, axis=0), pick)
    two = highest(jnp.concatenate(upper2, axis=0), pick)
    factor_ref[...] = highest(two, one)

    def finish(g, _):
        exchange(g, 1 - band).wait_send()

        @pl.when(band == 0)
        def _():
            exchange(g, 0).wait_send()

        for s in range(4):
            for d in range(4):
                @pl.when(sends[d])
                def _():
                    halo(d, s, g).wait_send()
        return 0

    lax.fori_loop(0, ng, finish, 0)


def filter_all(orbitals, potential):
    own = orbitals.shape[0]
    ng = own // 4
    field = pltpu.VMEM((ng, NY + 8, NXM, 8, NZ), jnp.float32)
    edges = pltpu.VMEM((4, ng, 4, 8, NZ), jnp.float32)
    return pl.pallas_call(
        functools.partial(kernel, ng),
        out_shape=(
            jax.ShapeDtypeStruct((own * 128, NZ), jnp.float32),
            jax.ShapeDtypeStruct((2 * own, 2 * own), jnp.float32),
        ),
        in_specs=[pl.BlockSpec(memory_space=pltpu.VMEM)] * 2,
        out_specs=[pl.BlockSpec(memory_space=pltpu.VMEM)] * 2,
        scratch_shapes=[
            pltpu.VMEM((2 * ng, NY, NXM, 8, NZ), jnp.float32),
            field, field, field, field, edges, edges, edges,
            pltpu.VMEM((NY, NXM, 8, NZ), jnp.float32),
            pltpu.VMEM((16 * ng, NZ), jnp.float32),
            pltpu.VMEM((16 * ng, NZ), jnp.float32),
            pltpu.VMEM((2, 8, 4 * ng, NZ), jnp.float32),
            pltpu.VMEM((2, 4, 4 * ng, NZ), jnp.float32),
            pltpu.SemaphoreType.DMA((4, 4, ng)),
            pltpu.SemaphoreType.DMA((4, 4, ng)),
            pltpu.SemaphoreType.DMA((ng, 2)),
            pltpu.SemaphoreType.DMA((ng, 2)),
            pltpu.SemaphoreType.DMA((2, 8)),
            pltpu.SemaphoreType.DMA((2, 8)),
            pltpu.SemaphoreType.DMA((2, 4)),
            pltpu.SemaphoreType.DMA((2, 4)),
        ],
        compiler_params=pltpu.CompilerParams(
            collective_id=0, has_side_effects=True, vmem_limit_bytes=50 * 1024 * 1024
        ),
    )(orbitals.reshape(own * 128, NZ), potential.reshape(128, NZ))


def shards(orbitals, potential):
    basis, factor = filter_all(orbitals, potential)
    return (basis.reshape(orbitals.shape), factor)


def solution(mesh):
    covered = mesh.shape["space"] == 16 and mesh.shape["band"] == 2
    return jax.shard_map(
        shards if covered else general_shards,
        mesh=mesh,
        in_specs=(P("band", "space", None, None, None), P("space", None, None, None)),
        out_specs=(P("band", "space", None, None, None), P()),
        check_vma=False,
    )
```

```python
import functools

import jax
import jax.numpy as jnp
from jax import lax
from jax.experimental import pallas as pl
from jax.experimental.pallas import tpu as pltpu
from jax.sharding import PartitionSpec as P

DEG = 4
LEAD = 2
MESH = pl.DeviceIdType.MESH

coefficients = (-205.0 / 72.0, 8.0 / 5.0, -1.0 / 5.0, 8.0 / 315.0, -1.0 / 560.0)
centre_value = 9.25
half_range = 4.75
filter_scale = 1.0 / 32.0


def shifted(block, axis, distance):
    devices = range(lax.axis_size(axis))
    route = [(i - distance, i) for i in devices if i - distance in devices]
    return lax.ppermute(block, axis, route)


def padded_along(field_in, axis_dim, stride, tile_count, coordinate):
    extent = field_in.shape[axis_dim]
    if tile_count == 1:
        widths = [(0, 0)] * field_in.ndim
        widths[axis_dim] = (4, 4)
        return jnp.pad(field_in, widths)
    top_layers = lax.slice_in_dim(field_in, extent - 4, extent, axis=axis_dim)
    bottom_layers = lax.slice_in_dim(field_in, 0, 4, axis=axis_dim)
    received = []
    for direction, portion, retain in (
        (1, top_layers, coordinate > 0),
        (-1, bottom_layers, coordinate < tile_count - 1),
    ):
        arrived = shifted(portion, "space", direction * stride)
        received.append(jnp.where(retain, arrived, jnp.zeros_like(arrived)))
    return jnp.concatenate([received[0], field_in, received[1]], axis=axis_dim)


def hamiltonian(field_in, potential, layout):
    total = 3.0 * coefficients[0] * field_in
    for axis_dim, stride, tile_count, coordinate in layout:
        padded = padded_along(field_in, axis_dim, stride, tile_count, coordinate)
        extent = field_in.shape[axis_dim]
        for offset in range(1, 5):
            upper = lax.slice_in_dim(padded, 4 + offset, 4 + offset + extent, axis=axis_dim)
            lower = lax.slice_in_dim(padded, 4 - offset, 4 - offset + extent, axis=axis_dim)
            total = total + coefficients[offset] * (upper + lower)
    return -0.5 * total + potential * field_in


def orthonormalize(flat, reduce_gram, total_cells, rows, own_count):
    count_orbs = flat.shape[0]
    identity = jnp.eye(count_orbs, dtype=jnp.float32)
    current = flat
    lowers = []
    for round_index in range(2):
        partial_gram = jnp.tensordot(
            current, current, axes=(tuple(range(1, current.ndim)),) * 2,
            precision=lax.Precision.HIGHEST, preferred_element_type=jnp.float32,
        )
        gram = reduce_gram(partial_gram) / total_cells
        lower = jnp.linalg.cholesky(gram)
        inverse = jax.scipy.linalg.solve_triangular(lower, identity, lower=True)
        if round_index == 1:
            inverse = lax.dynamic_slice_in_dim(inverse, rows, own_count, axis=0)
        current = jnp.tensordot(
            inverse, current, axes=1, precision=lax.Precision.HIGHEST, preferred_element_type=jnp.float32
        )
        lowers.append(lower)
    factor = jnp.dot(
        lowers[0], lowers[1], precision=lax.Precision.HIGHEST, preferred_element_type=jnp.float32
    ).T
    return (current, factor)


def reduce_everywhere(partial_gram):
    total = partial_gram
    size = lax.axis_size("space")
    step = 1
    while step < size:
        route = [(i, i ^ step) for i in range(size)]
        total = total + lax.ppermute(total, "space", route)
        step *= 2
    return total


def general_shards(orbitals, potential):
    tile_index = lax.axis_index("space")
    layout = (
        (2, 16, lax.axis_size("space") // 16, tile_index // 16),
        (3, 4, 4, tile_index // 4 % 4),
        (4, 1, 4, tile_index % 4),
    )
    previous = orbitals
    current = (hamiltonian(orbitals, potential, layout) - centre_value * orbitals) / half_range
    for step_index in range(DEG - 1):
        following = (
            2.0 * (hamiltonian(current, potential, layout) - centre_value * current) / half_range
            - previous
        )
        previous, current = (current, following)
    filtered = current * filter_scale
    own_count = filtered.shape[0]
    everything = lax.all_gather(filtered, "band", axis=0, tiled=True)
    total_cells = everything[0].size * lax.axis_size("space")
    rows = lax.axis_index("band") * own_count
    ortho, factor = orthonormalize(everything, reduce_everywhere, total_cells, rows, own_count)
    return (ortho.reshape(filtered.shape), factor)


NY, NXM, NZ = 16, 4, 128
ROWS = 16
UP, DOWN, LEFT, RIGHT = 0, 1, 2, 3


def kernel(
    ng, x_hbm, pot_ref, out_ref, factor_ref, x_ref, f_ref, y0, y1, y2, y3, pack, from_left, from_right, weight,
    stencil, twice, gram, spread, plane, column, send, recv, xsend, xrecv, psend, precv, csend, crecv, fetch,
):
    ys = (y0, y1, y2, y3)
    cells = 16 * 8 * NY * NZ
    t = lax.axis_index("space")
    band = lax.axis_index("band")
    ty, tz = t // 4, t % 4
    lane = lax.broadcasted_iota(jnp.int32, (8, NZ), 1)
    sub = lax.broadcasted_iota(jnp.int32, (8, NZ), 0)
    even = sub % 2 == 0
    zero = jnp.zeros((8, NZ), jnp.float32)
    seat = lane % 8
    wide_lane = lax.broadcasted_iota(jnp.int32, (16, NZ), 1) // 8
    wide_row = lax.broadcasted_iota(jnp.int32, (16, NZ), 0) // 8
    seats = [wide_lane == 2 * j + wide_row for j in range(ROWS // 2)]
    seats_next = [wide_lane == (2 * j + wide_row + 1) % 16 for j in range(ROWS // 2)]
    seats_last = [wide_lane == (2 * j + wide_row + 2) % 16 for j in range(ROWS // 2)]

    def dot(a, b):
        return jnp.dot(a, b, preferred_element_type=jnp.float32)

    def parts(a):
        high = a.astype(jnp.bfloat16)
        rest = a - high.astype(jnp.float32)
        middle = rest.astype(jnp.bfloat16)
        low = (rest - middle.astype(jnp.float32)).astype(jnp.bfloat16)
        return high, middle, low

    source = lax.broadcasted_iota(jnp.int32, (2 * NZ, NZ), 0)
    target = lax.broadcasted_iota(jnp.int32, (2 * NZ, NZ), 1)
    m = source % 8
    source = jnp.where(source < NZ, source, jnp.where(m < 4, m - 4, 124 + m))
    apart = jnp.abs(source - target)
    taps = jnp.zeros((2 * NZ, NZ), jnp.float32)
    for k in range(1, 5):
        taps = jnp.where(apart == k, float(round(5040 * coefficients[k])), taps)
    stencil[...] = taps.astype(jnp.bfloat16)
    twice[...] = jnp.concatenate([taps[0:NZ], taps[0:NZ]], axis=0).astype(jnp.bfloat16)

    sends = (ty > 0, ty < 3, tz > 0, tz < 3)
    gets = (ty < 3, ty > 0, tz < 3, tz > 0)
    offset = (-4, 4, -1, 1)

    def halo(d, s, g):
        if d == UP:
            src, dst = ys[s].at[g, pl.ds(4, 4)], ys[s].at[g, pl.ds(20, 4)]
        elif d == DOWN:
            src, dst = ys[s].at[g, pl.ds(16, 4)], ys[s].at[g, pl.ds(0, 4)]
        elif d == LEFT:
            src, dst = pack.at[s, g], from_right.at[s, g]
        else:
            src, dst = pack.at[s, g], from_left.at[s, g]
        return pltpu.make_async_remote_copy(
            src_ref=src, dst_ref=dst, send_sem=send.at[d], recv_sem=recv.at[d, s, g],
            device_id=(t + offset[d], band), device_id_type=MESH,
        )

    def exchange(g, half):
        part = f_ref.at[band * ng + g, pl.ds(8 * half, 8)]
        return pltpu.make_async_remote_copy(
            src_ref=part, dst_ref=part, send_sem=xsend.at[0], recv_sem=xrecv.at[g, half],
            device_id=(t, 1 - band), device_id_type=MESH,
        )

    def arrival(g, half):
        part = f_ref.at[(1 - band) * ng + g, pl.ds(8 * half, 8)]
        return pltpu.make_async_remote_copy(
            src_ref=part, dst_ref=part, send_sem=xsend.at[0], recv_sem=xrecv.at[g, half],
            device_id=(t, 1 - band), device_id_type=MESH,
        )

    def fetched(g):
        rows = pl.ds(g * 512, 512)
        return pltpu.make_async_copy(x_hbm.at[rows], x_ref.at[rows], fetch.at[g])

    for g in range(ng):
        fetched(g).start()

    def clear(step, _):
        for s in range(4):
            @pl.when(ty == 0)
            def _():
                ys[s][step, 0:4] = jnp.zeros((4, NXM, 8, NZ), jnp.float32)

            @pl.when(ty == 3)
            def _():
                ys[s][step, 20:24] = jnp.zeros((4, NXM, 8, NZ), jnp.float32)

            @pl.when(tz == 0)
            def _():
                from_left[s, step] = jnp.zeros((4, 8, NZ), jnp.float32)

            @pl.when(tz == 3)
            def _():
                from_right[s, step] = jnp.zeros((4, 8, NZ), jnp.float32)
        return 0

    seat_in_plane = band * 4 + tz

    def in_plane(step):
        other = (seat_in_plane + step) % 8
        return other, (4 * ty + other % 4, other // 4)

    def in_column(step):
        other = (ty + step) % 4
        return other, (4 * other + tz, band)

    barrier = pltpu.get_barrier_semaphore()
    for step in range(1, 8):
        pl.semaphore_signal(barrier, inc=1, device_id=in_plane(step)[1], device_id_type=MESH)
    for step in range(1, 4):
        pl.semaphore_signal(barrier, inc=1, device_id=in_column(step)[1], device_id_type=MESH)

    def weigh(y, _):
        for xm in range(NXM):
            low = pot_ref[pl.ds(xm * NY + y, 1), :]
            high = pot_ref[pl.ds((4 + xm) * NY + y, 1), :]
            both = jnp.where(even, jnp.broadcast_to(low, (8, NZ)), jnp.broadcast_to(high, (8, NZ)))
            weight[y, xm] = (2.0 / half_range) * (both - (1.5 * coefficients[0] + centre_value))
        return 0


    def start_halos(s, g):
        for d in range(4):
            @pl.when(sends[d])
            def _():
                halo(d, s, g).start()

    def prepare(g):
        def quad(q, _):
            packed = zero
            for j in range(ROWS):
                y, xm = 4 * q + j // 4, j % 4
                v = x_ref[pl.ds(g * 512 + xm * NY + y, 8, stride=64), :]
                y0[g, 4 + y, xm] = v
                packed = jnp.where(lane // 8 == j, pltpu.roll(v, 8 * j + 4, 1), packed)
            pack[0, g, q] = packed
            return 0

        fetched(g).wait()
        lax.fori_loop(0, 4, quad, 0)

    def unit(s, g):
        for d in (LEFT, RIGHT):
            @pl.when(gets[d])
            def _():
                halo(d, s, g).wait_recv()
        now = ys[s]
        scale = (1.0 if s == 0 else 2.0) / half_range * (filter_scale if s == 3 else 1.0)
        keep = filter_scale if s == 3 else 1.0
        ck = [None] + [-0.5 * scale * c for c in coefficients[1:]]

        def quad(i, _):
            q = (i + 1) % 4
            for turn_of, d in ((2, UP), (3, DOWN)):
                @pl.when((i == turn_of) & gets[d])
                def _():
                    halo(d, s, g).wait_recv()

            edges = jnp.where(seat < 4, from_left[s, g, q], from_right[s, g, q])
            fields = now[g, pl.ds(4 + 4 * q, 4)].reshape(8 * ROWS, NZ)
            along = None
            for part, edge in zip(parts(fields), parts(edges)):
                seated = [jnp.where(seats[j // 2], jnp.concatenate([edge, edge], axis=0), 0).astype(jnp.bfloat16)
                          for j in range(0, ROWS, 2)]
                both = jnp.concatenate([part, jnp.concatenate(seated, axis=0)], axis=1)
                term = jnp.dot(both, stencil[...], preferred_element_type=jnp.float32)
                along = term if along is None else along + term
            packed = zero
            for yy in range(4):
                y = 4 * q + yy
                v = [now[g, 4 + y, xm] for xm in range(NXM)]
                upper = [jnp.where(even, pltpu.roll(a, 7, 0), 0.0) for a in v]
                lower = [jnp.where(even, 0.0, pltpu.roll(a, 1, 0)) for a in v]
                for xm in range(NXM):
                    j = 4 * yy + xm
                    acc = (-0.5 * scale / 5040.0) * along[8 * j : 8 * j + 8]
                    for k in range(1, 5):
                        total = now[g, 4 + y - k, xm] + now[g, 4 + y + k, xm]
                        right = v[xm + k] if xm + k < 4 else upper[xm + k - 4]
                        left = v[xm - k] if xm >= k else lower[xm - k + 4]
                        acc = acc + ck[k] * (total + (right + left))
                    w = weight[y, xm]
                    if s == 0:
                        new = acc + 0.5 * w * v[xm]
                    elif s == 3:
                        new = acc + (keep * w) * v[xm] - keep * ys[s - 1][g, 4 + y, xm]
                    else:
                        new = acc + w * v[xm] - ys[s - 1][g, 4 + y, xm]
                    if s < 3:
                        ys[s + 1][g, 4 + y, xm] = new
                        packed = jnp.where(lane // 8 == j, pltpu.roll(new, (8 * j + 4) % NZ, 1), packed)
                    else:
                        f_ref[band * ng + g, y, xm] = new
            if s < 3:
                pack[s + 1, g, q] = packed
                for turn_of, d in ((2, DOWN), (3, UP)):
                    @pl.when((i == turn_of) & sends[d])
                    def _():
                        halo(d, s + 1, g).start()
            return 0

        lax.fori_loop(0, 4, quad, 0)
        if s < 3:
            for d in (LEFT, RIGHT):
                @pl.when(sends[d])
                def _():
                    halo(d, s + 1, g).start()
        else:
            exchange(g, 1 - band).start()

            @pl.when((band == 0) & (g >= 1) & (g < ng - 1))
            def _():
                exchange(g - 1, 0).start()

    lead = LEAD
    prepare(0)
    pl.semaphore_wait(barrier, 10)
    start_halos(0, 0)
    for g in range(1, lead):
        prepare(g)
        start_halos(0, g)
    lax.fori_loop(0, NY, weigh, 0)
    lax.fori_loop(0, ng, clear, 0)

    def turn(step, _):
        for s in (3, 2, 1, 0):
            g = step - s
            @pl.when((g >= 0) & (g < ng))
            def _():
                unit(s, g)

        @pl.when(step + lead < ng)
        def _():
            prepare(step + lead)
            start_halos(0, step + lead)
        return 0

    lax.fori_loop(0, ng + 3, turn, 0)

    def shares(g, _):
        arrival(g, band).wait_recv()
        return 0

    lax.fori_loop(0, ng, shares, 0)

    @pl.when(band == 0)
    def _():
        exchange(ng - 2, 0).start()
        exchange(ng - 1, 0).start()

    nr = 16 * ng
    norb = nr // 2
    tiles = norb // 8
    even_lane = lane % 2 == 0

    def block(y, xm):
        return f_ref[:, y, xm].reshape(nr, NZ)

    def line(y):
        return jnp.concatenate([block(y, xm) for xm in range(NXM)], axis=1)

    def inner(a):
        high, middle, low = parts(a)

        def dot_t(x, y):
            return lax.dot_general(x, y, (((1,), (1,)), ((), ())), preferred_element_type=jnp.float32)

        by_high = dot_t(jnp.concatenate([high, middle, low], axis=0), high)
        even_part = by_high[0:nr] + dot_t(middle, middle)
        return even_part, by_high[nr : 2 * nr] + by_high[2 * nr : 3 * nr]

    def apply_left(matrix_parts, a):
        m0, m1, m2 = matrix_parts
        a0, a1, a2 = parts(a)
        rows = m0.shape[0]
        lead = dot(
            jnp.concatenate([jnp.concatenate([m0, m0], axis=1), jnp.concatenate([m1, m1], axis=1)], axis=0),
            jnp.concatenate([a0, a1], axis=0),
        )
        rest = dot(jnp.concatenate([m2, m0], axis=1), jnp.concatenate([a0, a2], axis=0))
        return lead[0:rows] + (lead[rows:] + rest)

    def added(total, more):
        return total[0] + more[0], total[1] + more[1]

    def none():
        return jnp.zeros((nr, nr), jnp.float32), jnp.zeros((nr, nr), jnp.float32)

    def whole(total):
        return total[0] + (total[1] + total[1].T)

    def reduce_all(which, partial):
        gram[...] = jnp.zeros((nr, NZ), jnp.float32)
        gram[:, 0:nr] = partial
        first_half = gram[pl.ds(0, norb, stride=2), :]
        second_half = gram[pl.ds(1, norb, stride=2), :]
        both = [
            (first_half[8 * i : 8 * i + 8] + pltpu.roll(second_half[8 * i : 8 * i + 8], NZ - 1, 1)) * (1.0 / cells)
            for i in range(tiles)
        ]
        for i in range(tiles // 2):
            packed = jnp.where(even_lane, both[i], pltpu.roll(both[i + tiles // 2], 1, 1))
            plane[which, seat_in_plane, pl.ds(8 * i, 8)] = packed

        def to_plane(step):
            other, device = in_plane(step)
            mine = plane.at[which, seat_in_plane]
            return other, pltpu.make_async_remote_copy(
                src_ref=mine, dst_ref=mine, send_sem=psend.at[0], recv_sem=precv.at[which, seat_in_plane],
                device_id=device, device_id_type=MESH,
            )

        def from_plane(step):
            other, device = in_plane(step)
            theirs = plane.at[which, other]
            return pltpu.make_async_remote_copy(
                src_ref=theirs, dst_ref=theirs, send_sem=psend.at[0], recv_sem=precv.at[which, other],
                device_id=device, device_id_type=MESH,
            )

        def to_column(step):
            other, device = in_column(step)
            mine = column.at[which, ty]
            return pltpu.make_async_remote_copy(
                src_ref=mine, dst_ref=mine, send_sem=csend.at[0], recv_sem=crecv.at[which, ty],
                device_id=device, device_id_type=MESH,
            )

        def from_column(step):
            other, device = in_column(step)
            theirs = column.at[which, other]
            return pltpu.make_async_remote_copy(
                src_ref=theirs, dst_ref=theirs, send_sem=csend.at[0], recv_sem=crecv.at[which, other],
                device_id=device, device_id_type=MESH,
            )

        for step in range(1, 8):
            to_plane(step)[1].start()
        for step in range(1, 8):
            from_plane(step).wait_recv()
        for i in range(tiles // 2):
            column[which, ty, pl.ds(8 * i, 8)] = sum(plane[which, o, pl.ds(8 * i, 8)] for o in range(8))
        for step in range(1, 4):
            to_column(step).start()
        for step in range(1, 4):
            from_column(step).wait_recv()
        full = [sum(column[which, o, pl.ds(8 * i, 8)] for o in range(4)) for i in range(tiles // 2)]
        return [jnp.where(even_lane, a, pltpu.roll(a, 1, 1)) for a in full] + [
            jnp.where(even_lane, pltpu.roll(a, NZ - 1, 1), a) for a in full
        ]

    def eliminate(a, b):
        a, b = list(a), list(b)
        pivots = [zero + 1.0 for _ in range(tiles)]

        def across(v, j):
            return jnp.broadcast_to(v[:, 2 * j : 2 * j + 1], (8, NZ))

        for j in range(0, norb, 4):
            at, r = j // 8, j % 8
            row = [jnp.broadcast_to(a[at][r + k : r + k + 1, :], (8, NZ)) for k in range(4)]
            row_b = [jnp.broadcast_to(b[at][r + k : r + k + 1, :], (8, NZ)) for k in range(4)]
            cell = {(k, l): across(row[k], j + l) for k in range(4) for l in range(k + 1)}
            inverse = []
            for k in range(4):
                inverse.append(1.0 / cell[k, k])
                for l in range(k + 1, 4):
                    ratio = cell[l, k] * inverse[k]
                    for n in range(k + 1, l + 1):
                        cell[l, n] = cell[l, n] - ratio * cell[n, k]
                    row[l] = row[l] - ratio * row[k]
                    row_b[l] = row_b[l] - ratio * row_b[k]
            for i in range(at, tiles):
                if i == at and r == 4:
                    continue
                share = []
                for k in range(4):
                    col = across(a[i], j + k)
                    for l in range(k):
                        col = col - share[l] * cell[k, l]
                    share.append(col * inverse[k])
                if i == at:
                    share = [jnp.where(sub > r + 3, m, 0.0) for m in share]
                a[i] = a[i] - ((share[0] * row[0] + share[1] * row[1]) + (share[2] * row[2] + share[3] * row[3]))
                b[i] = b[i] - ((share[0] * row_b[0] + share[1] * row_b[1]) + (share[2] * row_b[2] + share[3] * row_b[3]))
            for k in range(4):
                a[at] = jnp.where(sub == r + k, row[k], a[at])
                b[at] = jnp.where(sub == r + k, row_b[k], b[at])
                pivots[at] = jnp.where(sub == r + k, cell[k, k], pivots[at])
        scale = [lax.rsqrt(p) for p in pivots]
        upper = [jnp.where(lane // 2 >= sub + 8 * i, a[i] * scale[i], 0.0) for i in range(tiles)]
        return upper, [b[i] * scale[i] for i in range(tiles)]

    def spread_rows(a):
        whole = jnp.concatenate(a, axis=0)
        is_even = jnp.concatenate([even_lane] * tiles, axis=0)
        spread[pl.ds(0, norb, stride=2), :] = jnp.where(is_even, whole, 0.0)
        spread[pl.ds(1, norb, stride=2), :] = jnp.where(is_even, 0.0, whole)

    def highest(a, b):
        return jnp.dot(a, b, precision=lax.Precision.HIGHEST, preferred_element_type=jnp.float32)

    def add_first(i, total):
        return added(total, inner(line(8 * band + i)))


    def run_tail():
        g1 = whole(lax.fori_loop(0, 8, add_first, none(), unroll=2))
        gram1 = reduce_all(0, g1)
        unit_rows = [jnp.where((lane // 2 == sub + 8 * i), 1.0, 0.0) for i in range(tiles)]
        upper1, inverse1 = eliminate(gram1, unit_rows)
        spread_rows(inverse1)

        left = parts(spread[:, 0:nr])

        def add_second(i, total):
            return added(total, inner(apply_left(left, line(8 * band + i))))
        g2 = whole(lax.fori_loop(0, 8, add_second, none(), unroll=2))
        gram2 = reduce_all(1, g2)
        upper2, inverse2 = eliminate(gram2, inverse1)
        spread_rows(inverse2)
        own = nr // 2
        @pl.when(band == 0)
        def _():
            def rows(i, _):
                y = i
                fields = jnp.concatenate([f_ref[0:ng, y, xm].reshape(own, NZ) for xm in range(NXM)], axis=1)
                result = apply_left(parts(spread[0:own, 0:own]), fields)
                for xm in range(NXM):
                    out_ref[pl.ds(xm * NY + y, own, stride=64), :] = result[:, NZ * xm : NZ * xm + NZ]
                return 0

            lax.fori_loop(0, NY, rows, 0, unroll=2)

        @pl.when(band == 1)
        def _():
            def late(g, _):
                arrival(g, 0).wait_recv()
                return 0

            lax.fori_loop(0, ng, late, 0)

            def rows(i, _):
                result = apply_left(parts(spread[own:nr, 0:nr]), line(i))
                for xm in range(NXM):
                    out_ref[pl.ds(xm * NY + i, own, stride=64), :] = result[:, NZ * xm : NZ * xm + NZ]
                return 0

            lax.fori_loop(0, NY, rows, 0, unroll=2)

        pick = jnp.where(
            lax.broadcasted_iota(jnp.int32, (NZ, norb), 0) == 2 * lax.broadcasted_iota(jnp.int32, (NZ, norb), 1), 1.0, 0.0
        )
        one = highest(jnp.concatenate(upper1, axis=0), pick)
        two = highest(jnp.concatenate(upper2, axis=0), pick)
        factor_ref[...] = highest(two, one)


    run_tail()
    for sem, whole_of in ((psend, plane.at[:, pl.ds(0, 7)]), (csend, column.at[:, pl.ds(0, 3)])):
        pltpu.make_async_remote_copy(
            src_ref=whole_of, dst_ref=whole_of, send_sem=sem.at[0], recv_sem=precv.at[0, 0],
            device_id=(t, 1 - band), device_id_type=MESH,
        ).wait_send()
    for d in range(4):
        everything = y0.at[:, pl.ds(0, 16)] if d < 2 else pack
        @pl.when(sends[d])
        def _():
            pltpu.make_async_remote_copy(
                src_ref=everything, dst_ref=everything, send_sem=send.at[d], recv_sem=recv.at[d, 0, 0],
                device_id=(t + offset[d], band), device_id_type=MESH,
            ).wait_send()

    def sent(whole):
        pltpu.make_async_remote_copy(
            src_ref=whole, dst_ref=whole, send_sem=xsend.at[0], recv_sem=xrecv.at[0, 0],
            device_id=(t, 1 - band), device_id_type=MESH,
        ).wait_send()

    @pl.when(band == 0)
    def _():
        sent(f_ref.at[pl.ds(0, ng)])

    @pl.when(band == 1)
    def _():
        sent(f_ref.at[pl.ds(0, ng), pl.ds(0, 8)])


def filter_all(orbitals, potential):
    own = orbitals.shape[0]
    ng = own // 4
    field = pltpu.VMEM((ng, NY + 8, NXM, 8, NZ), jnp.float32)
    edges = pltpu.VMEM((4, ng, 4, 8, NZ), jnp.float32)
    return pl.pallas_call(
        functools.partial(kernel, ng),
        out_shape=(
            jax.ShapeDtypeStruct((own * 128, NZ), jnp.float32),
            jax.ShapeDtypeStruct((2 * own, 2 * own), jnp.float32),
        ),
        in_specs=[pl.BlockSpec(memory_space=pl.ANY), pl.BlockSpec(memory_space=pltpu.VMEM)],
        out_specs=[pl.BlockSpec(memory_space=pltpu.VMEM)] * 2,
        scratch_shapes=[
            pltpu.VMEM((own * 128, NZ), jnp.float32),
            pltpu.VMEM((2 * ng, NY, NXM, 8, NZ), jnp.float32),
            field, field, field, field, edges, edges, edges,
            pltpu.VMEM((NY, NXM, 8, NZ), jnp.float32),
            pltpu.VMEM((2 * NZ, NZ), jnp.bfloat16),
            pltpu.VMEM((2 * NZ, NZ), jnp.bfloat16),
            pltpu.VMEM((16 * ng, NZ), jnp.float32),
            pltpu.VMEM((16 * ng, NZ), jnp.float32),
            pltpu.VMEM((2, 8, 4 * ng, NZ), jnp.float32),
            pltpu.VMEM((2, 4, 4 * ng, NZ), jnp.float32),
            pltpu.SemaphoreType.DMA((4,)),
            pltpu.SemaphoreType.DMA((4, 4, ng)),
            pltpu.SemaphoreType.DMA((1,)),
            pltpu.SemaphoreType.DMA((ng, 2)),
            pltpu.SemaphoreType.DMA((1,)),
            pltpu.SemaphoreType.DMA((2, 8)),
            pltpu.SemaphoreType.DMA((1,)),
            pltpu.SemaphoreType.DMA((2, 4)),
            pltpu.SemaphoreType.DMA((ng,)),
        ],
        compiler_params=pltpu.CompilerParams(
            collective_id=0, has_side_effects=True, vmem_limit_bytes=50 * 1024 * 1024
        ),
    )(orbitals.reshape(own * 128, NZ), potential.reshape(128, NZ))


def shards(orbitals, potential):
    basis, factor = filter_all(orbitals, potential)
    return (basis.reshape(orbitals.shape), factor)


def solution(mesh):
    covered = mesh.shape["space"] == 16 and mesh.shape["band"] == 2
    return jax.shard_map(
        shards if covered else general_shards,
        mesh=mesh,
        in_specs=(P("band", "space", None, None, None), P("space", None, None, None)),
        out_specs=(P("band", "space", None, None, None), P()),
        check_vma=False,
    )
```

```python
import functools

import jax
import jax.numpy as jnp
from jax import lax
from jax.experimental import pallas as pl
from jax.experimental.pallas import tpu as pltpu
from jax.sharding import PartitionSpec as P

DEG = 4
LAG, LEAD = 2, 3
LATE0 = 1
LATE1 = 8
MESH = pl.DeviceIdType.MESH

coefficients = (-205.0 / 72.0, 8.0 / 5.0, -1.0 / 5.0, 8.0 / 315.0, -1.0 / 560.0)
centre_value = 9.25
half_range = 4.75
filter_scale = 1.0 / 32.0


def shifted(block, axis, distance):
    devices = range(lax.axis_size(axis))
    route = [(i - distance, i) for i in devices if i - distance in devices]
    return lax.ppermute(block, axis, route)


def padded_along(field_in, axis_dim, stride, tile_count, coordinate):
    extent = field_in.shape[axis_dim]
    if tile_count == 1:
        widths = [(0, 0)] * field_in.ndim
        widths[axis_dim] = (4, 4)
        return jnp.pad(field_in, widths)
    top_layers = lax.slice_in_dim(field_in, extent - 4, extent, axis=axis_dim)
    bottom_layers = lax.slice_in_dim(field_in, 0, 4, axis=axis_dim)
    received = []
    for direction, portion, retain in (
        (1, top_layers, coordinate > 0),
        (-1, bottom_layers, coordinate < tile_count - 1),
    ):
        arrived = shifted(portion, "space", direction * stride)
        received.append(jnp.where(retain, arrived, jnp.zeros_like(arrived)))
    return jnp.concatenate([received[0], field_in, received[1]], axis=axis_dim)


def hamiltonian(field_in, potential, layout):
    total = 3.0 * coefficients[0] * field_in
    for axis_dim, stride, tile_count, coordinate in layout:
        padded = padded_along(field_in, axis_dim, stride, tile_count, coordinate)
        extent = field_in.shape[axis_dim]
        for offset in range(1, 5):
            upper = lax.slice_in_dim(padded, 4 + offset, 4 + offset + extent, axis=axis_dim)
            lower = lax.slice_in_dim(padded, 4 - offset, 4 - offset + extent, axis=axis_dim)
            total = total + coefficients[offset] * (upper + lower)
    return -0.5 * total + potential * field_in


def orthonormalize(flat, reduce_gram, total_cells, rows, own_count):
    count_orbs = flat.shape[0]
    identity = jnp.eye(count_orbs, dtype=jnp.float32)
    current = flat
    lowers = []
    for round_index in range(2):
        partial_gram = jnp.tensordot(
            current, current, axes=(tuple(range(1, current.ndim)),) * 2,
            precision=lax.Precision.HIGHEST, preferred_element_type=jnp.float32,
        )
        gram = reduce_gram(partial_gram) / total_cells
        lower = jnp.linalg.cholesky(gram)
        inverse = jax.scipy.linalg.solve_triangular(lower, identity, lower=True)
        if round_index == 1:
            inverse = lax.dynamic_slice_in_dim(inverse, rows, own_count, axis=0)
        current = jnp.tensordot(
            inverse, current, axes=1, precision=lax.Precision.HIGHEST, preferred_element_type=jnp.float32
        )
        lowers.append(lower)
    factor = jnp.dot(
        lowers[0], lowers[1], precision=lax.Precision.HIGHEST, preferred_element_type=jnp.float32
    ).T
    return (current, factor)


def reduce_everywhere(partial_gram):
    total = partial_gram
    size = lax.axis_size("space")
    step = 1
    while step < size:
        route = [(i, i ^ step) for i in range(size)]
        total = total + lax.ppermute(total, "space", route)
        step *= 2
    return total


def general_shards(orbitals, potential):
    tile_index = lax.axis_index("space")
    layout = (
        (2, 16, lax.axis_size("space") // 16, tile_index // 16),
        (3, 4, 4, tile_index // 4 % 4),
        (4, 1, 4, tile_index % 4),
    )
    previous = orbitals
    current = (hamiltonian(orbitals, potential, layout) - centre_value * orbitals) / half_range
    for step_index in range(DEG - 1):
        following = (
            2.0 * (hamiltonian(current, potential, layout) - centre_value * current) / half_range
            - previous
        )
        previous, current = (current, following)
    filtered = current * filter_scale
    own_count = filtered.shape[0]
    everything = lax.all_gather(filtered, "band", axis=0, tiled=True)
    total_cells = everything[0].size * lax.axis_size("space")
    rows = lax.axis_index("band") * own_count
    ortho, factor = orthonormalize(everything, reduce_everywhere, total_cells, rows, own_count)
    return (ortho.reshape(filtered.shape), factor)


NY, NXM, NZ = 16, 4, 128
ROWS = 16
UP, DOWN, LEFT, RIGHT = 0, 1, 2, 3


def kernel(
    ng, x_hbm, pot_ref, out_ref, factor_ref, x_ref, f_ref, y0, y1, y2, y3, pack, from_left, from_right, weight,
    stencil, along, lower_ref, gram, spread, plane, column, send, recv, xsend, xrecv, psend, precv, csend, crecv, fetch,
):
    ys = (y0, y1, y2, y3)
    cells = 16 * 8 * NY * NZ
    t = lax.axis_index("space")
    band = lax.axis_index("band")
    ty, tz = t // 4, t % 4
    lane = lax.broadcasted_iota(jnp.int32, (8, NZ), 1)
    sub = lax.broadcasted_iota(jnp.int32, (8, NZ), 0)
    even = sub % 2 == 0
    zero = jnp.zeros((8, NZ), jnp.float32)
    seat = lane % 8
    wide_lane = lax.broadcasted_iota(jnp.int32, (16, NZ), 1) // 8
    wide_row = lax.broadcasted_iota(jnp.int32, (16, NZ), 0) // 8
    seats = [wide_lane == 2 * j + wide_row for j in range(ROWS // 2)]

    def dot(a, b):
        return jnp.dot(a, b, preferred_element_type=jnp.float32)

    def parts(a):
        high = a.astype(jnp.bfloat16)
        rest = a - high.astype(jnp.float32)
        middle = rest.astype(jnp.bfloat16)
        low = (rest - middle.astype(jnp.float32)).astype(jnp.bfloat16)
        return high, middle, low

    source = lax.broadcasted_iota(jnp.int32, (2 * NZ, NZ), 0)
    target = lax.broadcasted_iota(jnp.int32, (2 * NZ, NZ), 1)
    m = source % 8
    source = jnp.where(source < NZ, source, jnp.where(m < 4, m - 4, 124 + m))
    apart = jnp.abs(source - target)
    taps = jnp.zeros((2 * NZ, NZ), jnp.float32)
    for k in range(1, 5):
        taps = jnp.where(apart == k, float(round(5040 * coefficients[k])), taps)
    stencil[...] = taps.astype(jnp.bfloat16)

    sends = (ty > 0, ty < 3, tz > 0, tz < 3)
    gets = (ty < 3, ty > 0, tz < 3, tz > 0)
    offset = (-4, 4, -1, 1)

    def halo(d, s, g):
        if d == UP:
            src, dst = ys[s].at[g, pl.ds(4, 4)], ys[s].at[g, pl.ds(20, 4)]
        elif d == DOWN:
            src, dst = ys[s].at[g, pl.ds(16, 4)], ys[s].at[g, pl.ds(0, 4)]
        elif d == LEFT:
            src, dst = pack.at[s, g], from_right.at[s, g]
        else:
            src, dst = pack.at[s, g], from_left.at[s, g]
        return pltpu.make_async_remote_copy(
            src_ref=src, dst_ref=dst, send_sem=send.at[d], recv_sem=recv.at[d, s, g],
            device_id=(t + offset[d], band), device_id_type=MESH,
        )

    def exchange(g, half):
        part = f_ref.at[band * ng + g, pl.ds(8 * half, 8)]
        return pltpu.make_async_remote_copy(
            src_ref=part, dst_ref=part, send_sem=xsend.at[0], recv_sem=xrecv.at[g, half],
            device_id=(t, 1 - band), device_id_type=MESH,
        )

    def arrival(g, half):
        part = f_ref.at[(1 - band) * ng + g, pl.ds(8 * half, 8)]
        return pltpu.make_async_remote_copy(
            src_ref=part, dst_ref=part, send_sem=xsend.at[0], recv_sem=xrecv.at[g, half],
            device_id=(t, 1 - band), device_id_type=MESH,
        )

    def fetched(g):
        rows = pl.ds(g * 512, 512)
        return pltpu.make_async_copy(x_hbm.at[rows], x_ref.at[rows], fetch.at[g])

    for g in range(ng):
        fetched(g).start()

    def clear(step, _):
        for s in range(4):
            @pl.when(ty == 0)
            def _():
                ys[s][step, 0:4] = jnp.zeros((4, NXM, 8, NZ), jnp.float32)

            @pl.when(ty == 3)
            def _():
                ys[s][step, 20:24] = jnp.zeros((4, NXM, 8, NZ), jnp.float32)

            @pl.when(tz == 0)
            def _():
                from_left[s, step] = jnp.zeros((4, 8, NZ), jnp.float32)

            @pl.when(tz == 3)
            def _():
                from_right[s, step] = jnp.zeros((4, 8, NZ), jnp.float32)
        return 0

    seat_in_plane = band * 4 + tz

    def in_plane(step):
        other = (seat_in_plane + step) % 8
        return other, (4 * ty + other % 4, other // 4)

    def in_column(step):
        other = (ty + step) % 4
        return other, (4 * other + tz, band)

    barrier = pltpu.get_barrier_semaphore()
    for step in range(1, 8):
        pl.semaphore_signal(barrier, inc=1, device_id=in_plane(step)[1], device_id_type=MESH)
    for step in range(1, 4):
        pl.semaphore_signal(barrier, inc=1, device_id=in_column(step)[1], device_id_type=MESH)

    def weigh(y, _):
        for xm in range(NXM):
            low = pot_ref[pl.ds(xm * NY + y, 1), :]
            high = pot_ref[pl.ds((4 + xm) * NY + y, 1), :]
            both = jnp.where(even, jnp.broadcast_to(low, (8, NZ)), jnp.broadcast_to(high, (8, NZ)))
            weight[y, xm] = (2.0 / half_range) * (both - (1.5 * coefficients[0] + centre_value))
        return 0


    def start_halos(s, g):
        for d in range(4):
            @pl.when(sends[d])
            def _():
                halo(d, s, g).start()

    def pack_edges(s, g):
        for q in range(4):
            packed = zero
            for j in range(ROWS):
                moved = pltpu.roll(ys[s][g, 4 + 4 * q + j // 4, j % 4], (8 * j + 4) % NZ, 1)
                packed = jnp.where(lane // 8 == j, moved, packed)
            pack[s, g, q] = packed

    def along_z(s, g):
        total = None
        inside = parts(ys[s][g, pl.ds(4, NY)].reshape(NY * NXM * 8, NZ))
        edges = [parts(jnp.where(seat < 4, from_left[s, g, q], from_right[s, g, q])) for q in range(4)]
        for which in range(3):
            seated = [
                jnp.where(seats[j], jnp.concatenate([edges[q][which]] * 2, axis=0), jnp.bfloat16(0))
                for q in range(4) for j in range(ROWS // 2)
            ]
            both = jnp.concatenate([inside[which], jnp.concatenate(seated, axis=0)], axis=1)
            term = dot(both, stencil[...])
            total = term if total is None else total + term
        along[...] = total.reshape(NY, NXM, 8, NZ)

    def prepare(g):
        fetched(g).wait()

        def quad(q, _):
            for j in range(ROWS):
                y, xm = 4 * q + j // 4, j % 4
                y0[g, 4 + y, xm] = x_ref[pl.ds(g * 512 + xm * NY + y, 8, stride=64), :]
            return 0

        lax.fori_loop(0, 4, quad, 0)
        pack_edges(0, g)

    def unit(s, g):
        for d in (LEFT, RIGHT):
            @pl.when(gets[d])
            def _():
                halo(d, s, g).wait_recv()
        now = ys[s]
        scale = (1.0 if s == 0 else 2.0) / half_range * (filter_scale if s == 3 else 1.0)
        keep = filter_scale if s == 3 else 1.0
        ck = [None] + [-0.5 * scale * c for c in coefficients[1:]]
        along_z(s, g)

        def quad(i, _):
            q = (i + 1) % 4
            for turn_of, d in ((2, UP), (3, DOWN)):
                @pl.when((i == turn_of) & gets[d])
                def _():
                    halo(d, s, g).wait_recv()

            for yy in range(4):
                y = 4 * q + yy
                v = [now[g, 4 + y, xm] for xm in range(NXM)]
                upper = [jnp.where(even, pltpu.roll(a, 7, 0), 0.0) for a in v]
                lower = [jnp.where(even, 0.0, pltpu.roll(a, 1, 0)) for a in v]
                for xm in range(NXM):
                    acc = (-0.5 * scale / 5040.0) * along[y, xm]
                    for k in range(1, 5):
                        total = now[g, 4 + y - k, xm] + now[g, 4 + y + k, xm]
                        right = v[xm + k] if xm + k < 4 else upper[xm + k - 4]
                        left = v[xm - k] if xm >= k else lower[xm - k + 4]
                        acc = acc + ck[k] * (total + (right + left))
                    w = weight[y, xm]
                    if s == 0:
                        new = acc + 0.5 * w * v[xm]
                    elif s == 3:
                        new = acc + (keep * w) * v[xm] - keep * ys[s - 1][g, 4 + y, xm]
                    else:
                        new = acc + w * v[xm] - ys[s - 1][g, 4 + y, xm]
                    if s < 3:
                        ys[s + 1][g, 4 + y, xm] = new
                    else:
                        f_ref[band * ng + g, y, xm] = new
            if s < 3:
                for turn_of, d in ((2, DOWN), (3, UP)):
                    @pl.when((i == turn_of) & sends[d])
                    def _():
                        halo(d, s + 1, g).start()
            return 0

        lax.fori_loop(0, 4, quad, 0)
        if s < 3:
            pack_edges(s + 1, g)
            for d in (LEFT, RIGHT):
                @pl.when(sends[d])
                def _():
                    halo(d, s + 1, g).start()
        else:
            exchange(g, 1 - band).start()

    lead = LEAD
    prepare(0)
    pl.semaphore_wait(barrier, 10)
    start_halos(0, 0)
    for g in range(1, lead):
        prepare(g)
        start_halos(0, g)
    lax.fori_loop(0, NY, weigh, 0)
    lax.fori_loop(0, ng, clear, 0)

    def turn(step, _):
        for s in (3, 2, 1, 0):
            g = step - LAG * s
            @pl.when((g >= 0) & (g < ng))
            def _():
                unit(s, g)

        @pl.when(step + lead < ng)
        def _():
            prepare(step + lead)
            start_halos(0, step + lead)
        return 0

    lax.fori_loop(0, ng + 3 * LAG, turn, 0)

    def shares(g, _):
        arrival(g, band).wait_recv()
        return 0

    lax.fori_loop(0, ng, shares, 0)

    def start_late(first, last):
        @pl.when(band == 0)
        def _():
            for piece in range(first, last):
                part = f_ref.at[piece // 2, pl.ds(4 * (piece % 2), 4)]
                pltpu.make_async_remote_copy(
                    src_ref=part, dst_ref=part, send_sem=xsend.at[0], recv_sem=xrecv.at[piece // 2, 0],
                    device_id=(t, 1 - band), device_id_type=MESH,
                ).start()

    start_late(0, LATE0)

    nr = 16 * ng
    norb = nr // 2
    tiles = norb // 8
    even_lane = lane % 2 == 0

    def block(y, xm):
        return f_ref[:, y, xm].reshape(nr, NZ)

    def line(y):
        return jnp.concatenate([block(y, xm) for xm in range(NXM)], axis=1)

    def inner(a):
        high, middle, low = parts(a)

        def dot_t(x, y):
            return lax.dot_general(x, y, (((1,), (1,)), ((), ())), preferred_element_type=jnp.float32)

        by_high = dot_t(jnp.concatenate([high, middle, low], axis=0), high)
        even_part = by_high[0:nr] + dot_t(middle, middle)
        return even_part, by_high[nr : 2 * nr] + by_high[2 * nr : 3 * nr]

    def apply_left(matrix_parts, a):
        m0, m1, m2 = matrix_parts
        a0, a1, a2 = parts(a)
        rows = m0.shape[0]
        lead = dot(
            jnp.concatenate([jnp.concatenate([m0, m0], axis=1), jnp.concatenate([m1, m1], axis=1)], axis=0),
            jnp.concatenate([a0, a1], axis=0),
        )
        rest = dot(jnp.concatenate([m2, m0], axis=1), jnp.concatenate([a0, a2], axis=0))
        return lead[0:rows] + (lead[rows:] + rest)

    def added(total, more):
        return total[0] + more[0], total[1] + more[1]

    def none():
        return jnp.zeros((nr, nr), jnp.float32), jnp.zeros((nr, nr), jnp.float32)

    def whole(total):
        return total[0] + (total[1] + total[1].T)

    def reduce_all(which, partial, meanwhile=lambda: None):
        gram[...] = jnp.zeros((nr, NZ), jnp.float32)
        gram[:, 0:nr] = partial
        first_half = gram[pl.ds(0, norb, stride=2), :]
        second_half = gram[pl.ds(1, norb, stride=2), :]
        both = [
            (first_half[8 * i : 8 * i + 8] + pltpu.roll(second_half[8 * i : 8 * i + 8], NZ - 1, 1)) * (1.0 / cells)
            for i in range(tiles)
        ]
        for i in range(tiles // 2):
            packed = jnp.where(even_lane, both[i], pltpu.roll(both[i + tiles // 2], 1, 1))
            plane[which, seat_in_plane, pl.ds(8 * i, 8)] = packed

        def to_plane(step):
            other, device = in_plane(step)
            mine = plane.at[which, seat_in_plane]
            return other, pltpu.make_async_remote_copy(
                src_ref=mine, dst_ref=mine, send_sem=psend.at[0], recv_sem=precv.at[which, seat_in_plane],
                device_id=device, device_id_type=MESH,
            )

        def from_plane(step):
            other, device = in_plane(step)
            theirs = plane.at[which, other]
            return pltpu.make_async_remote_copy(
                src_ref=theirs, dst_ref=theirs, send_sem=psend.at[0], recv_sem=precv.at[which, other],
                device_id=device, device_id_type=MESH,
            )

        def to_column(step):
            other, device = in_column(step)
            mine = column.at[which, ty]
            return pltpu.make_async_remote_copy(
                src_ref=mine, dst_ref=mine, send_sem=csend.at[0], recv_sem=crecv.at[which, ty],
                device_id=device, device_id_type=MESH,
            )

        def from_column(step):
            other, device = in_column(step)
            theirs = column.at[which, other]
            return pltpu.make_async_remote_copy(
                src_ref=theirs, dst_ref=theirs, send_sem=csend.at[0], recv_sem=crecv.at[which, other],
                device_id=device, device_id_type=MESH,
            )

        for step in range(1, 8):
            to_plane(step)[1].start()
        meanwhile()
        for step in range(1, 8):
            from_plane(step).wait_recv()
        start_late(LATE0 if which == 0 else LATE1, LATE1 if which == 0 else 2 * ng)
        for i in range(tiles // 2):
            column[which, ty, pl.ds(8 * i, 8)] = sum(plane[which, o, pl.ds(8 * i, 8)] for o in range(8))
        for step in range(1, 4):
            to_column(step).start()
        for step in range(1, 4):
            from_column(step).wait_recv()
        full = [sum(column[which, o, pl.ds(8 * i, 8)] for o in range(4)) for i in range(tiles // 2)]
        return [jnp.where(even_lane, a, pltpu.roll(a, 1, 1)) for a in full] + [
            jnp.where(even_lane, pltpu.roll(a, NZ - 1, 1), a) for a in full
        ]

    def eliminate(a, b):
        a, b = list(a), list(b)
        pivots = [zero + 1.0 for _ in range(tiles)]

        def across(v, j):
            return jnp.broadcast_to(v[:, 2 * j : 2 * j + 1], (8, NZ))

        for j in range(0, norb, 4):
            at, r = j // 8, j % 8
            row = [jnp.broadcast_to(a[at][r + k : r + k + 1, :], (8, NZ)) for k in range(4)]
            row_b = [jnp.broadcast_to(b[at][r + k : r + k + 1, :], (8, NZ)) for k in range(4)]
            cell = {(k, l): across(row[k], j + l) for k in range(4) for l in range(k + 1)}
            inverse = []
            for k in range(4):
                inverse.append(1.0 / cell[k, k])
                for l in range(k + 1, 4):
                    ratio = cell[l, k] * inverse[k]
                    for n in range(k + 1, l + 1):
                        cell[l, n] = cell[l, n] - ratio * cell[n, k]
                    row[l] = row[l] - ratio * row[k]
                    row_b[l] = row_b[l] - ratio * row_b[k]
            for i in range(at, tiles):
                if i == at and r == 4:
                    continue
                share = []
                for k in range(4):
                    col = across(a[i], j + k)
                    for l in range(k):
                        col = col - share[l] * cell[k, l]
                    share.append(col * inverse[k])
                if i == at:
                    share = [jnp.where(sub > r + 3, m, 0.0) for m in share]
                a[i] = a[i] - ((share[0] * row[0] + share[1] * row[1]) + (share[2] * row[2] + share[3] * row[3]))
                b[i] = b[i] - ((share[0] * row_b[0] + share[1] * row_b[1]) + (share[2] * row_b[2] + share[3] * row_b[3]))
            for k in range(4):
                a[at] = jnp.where(sub == r + k, row[k], a[at])
                b[at] = jnp.where(sub == r + k, row_b[k], b[at])
                pivots[at] = jnp.where(sub == r + k, cell[k, k], pivots[at])
        scale = [lax.rsqrt(p) for p in pivots]
        upper = [jnp.where(lane // 2 >= sub + 8 * i, a[i] * scale[i], 0.0) for i in range(tiles)]
        return upper, [b[i] * scale[i] for i in range(tiles)]

    def spread_rows(a):
        whole = jnp.concatenate(a, axis=0)
        is_even = jnp.concatenate([even_lane] * tiles, axis=0)
        spread[pl.ds(0, norb, stride=2), :] = jnp.where(is_even, whole, 0.0)
        spread[pl.ds(1, norb, stride=2), :] = jnp.where(is_even, 0.0, whole)

    def highest(a, b):
        return jnp.dot(a, b, precision=lax.Precision.HIGHEST, preferred_element_type=jnp.float32)

    def add_first(i, total):
        return added(total, inner(line(8 * band + i)))


    pick = jnp.where(
        lax.broadcasted_iota(jnp.int32, (NZ, norb), 0) == 2 * lax.broadcasted_iota(jnp.int32, (NZ, norb), 1), 1.0, 0.0
    )

    def run_tail():
        g1 = whole(lax.fori_loop(0, 8, add_first, none(), unroll=4))
        gram1 = reduce_all(0, g1)
        unit_rows = [jnp.where((lane // 2 == sub + 8 * i), 1.0, 0.0) for i in range(tiles)]
        upper1, inverse1 = eliminate(gram1, unit_rows)
        spread_rows(inverse1)

        left = parts(spread[:, 0:nr])

        def add_second(i, total):
            return added(total, inner(apply_left(left, line(8 * band + i))))
        g2 = whole(lax.fori_loop(0, 8, add_second, none(), unroll=4))
        def first_factor():
            lower_ref[...] = highest(jnp.concatenate(upper1, axis=0), pick)

        gram2 = reduce_all(1, g2, first_factor)
        upper2, inverse2 = eliminate(gram2, inverse1)
        spread_rows(inverse2)
        own = nr // 2
        factor_ref[...] = highest(highest(jnp.concatenate(upper2, axis=0), pick), lower_ref[...])
        @pl.when(band == 0)
        def _():
            def rows(i, _):
                y = i
                fields = jnp.concatenate([f_ref[0:ng, y, xm].reshape(own, NZ) for xm in range(NXM)], axis=1)
                result = apply_left(parts(spread[0:own, 0:own]), fields)
                for xm in range(NXM):
                    out_ref[pl.ds(xm * NY + y, own, stride=64), :] = result[:, NZ * xm : NZ * xm + NZ]
                return 0

            lax.fori_loop(0, NY, rows, 0, unroll=4)

        @pl.when(band == 1)
        def _():
            def rows(i, _):
                result = apply_left(parts(spread[own:nr, 0:nr]), line(i))
                for xm in range(NXM):
                    out_ref[pl.ds(xm * NY + i, own, stride=64), :] = result[:, NZ * xm : NZ * xm + NZ]
                return 0

            def late(g, _):
                arrival(g, 0).wait_recv()
                return 0

            lax.fori_loop(NY // 2, NY, rows, 0, unroll=4)
            lax.fori_loop(0, ng, late, 0)
            lax.fori_loop(0, NY // 2, rows, 0, unroll=4)

    run_tail()
    for sem, whole_of in ((psend, plane.at[:, pl.ds(0, 7)]), (csend, column.at[:, pl.ds(0, 3)])):
        pltpu.make_async_remote_copy(
            src_ref=whole_of, dst_ref=whole_of, send_sem=sem.at[0], recv_sem=precv.at[0, 0],
            device_id=(t, 1 - band), device_id_type=MESH,
        ).wait_send()
    for d in range(4):
        everything = y0.at[:, pl.ds(0, 16)] if d < 2 else pack
        @pl.when(sends[d])
        def _():
            pltpu.make_async_remote_copy(
                src_ref=everything, dst_ref=everything, send_sem=send.at[d], recv_sem=recv.at[d, 0, 0],
                device_id=(t + offset[d], band), device_id_type=MESH,
            ).wait_send()

    def sent(whole):
        pltpu.make_async_remote_copy(
            src_ref=whole, dst_ref=whole, send_sem=xsend.at[0], recv_sem=xrecv.at[0, 0],
            device_id=(t, 1 - band), device_id_type=MESH,
        ).wait_send()

    @pl.when(band == 0)
    def _():
        sent(f_ref.at[pl.ds(0, ng)])

    @pl.when(band == 1)
    def _():
        sent(f_ref.at[pl.ds(0, ng), pl.ds(0, 8)])


def filter_all(orbitals, potential):
    own = orbitals.shape[0]
    ng = own // 4
    field = pltpu.VMEM((ng, NY + 8, NXM, 8, NZ), jnp.float32)
    edges = pltpu.VMEM((4, ng, 4, 8, NZ), jnp.float32)
    return pl.pallas_call(
        functools.partial(kernel, ng),
        out_shape=(
            jax.ShapeDtypeStruct((own * 128, NZ), jnp.float32),
            jax.ShapeDtypeStruct((2 * own, 2 * own), jnp.float32),
        ),
        in_specs=[pl.BlockSpec(memory_space=pltpu.HBM), pl.BlockSpec(memory_space=pltpu.VMEM)],
        out_specs=[pl.BlockSpec(memory_space=pltpu.VMEM)] * 2,
        scratch_shapes=[
            pltpu.VMEM((own * 128, NZ), jnp.float32),
            pltpu.VMEM((2 * ng, NY, NXM, 8, NZ), jnp.float32),
            field, field, field, field, edges, edges, edges,
            pltpu.VMEM((NY, NXM, 8, NZ), jnp.float32),
            pltpu.VMEM((2 * NZ, NZ), jnp.bfloat16),
            pltpu.VMEM((NY, NXM, 8, NZ), jnp.float32),
            pltpu.VMEM((8 * ng, 8 * ng), jnp.float32),
            pltpu.VMEM((16 * ng, NZ), jnp.float32),
            pltpu.VMEM((16 * ng, NZ), jnp.float32),
            pltpu.VMEM((2, 8, 4 * ng, NZ), jnp.float32),
            pltpu.VMEM((2, 4, 4 * ng, NZ), jnp.float32),
            pltpu.SemaphoreType.DMA((4,)),
            pltpu.SemaphoreType.DMA((4, 4, ng)),
            pltpu.SemaphoreType.DMA((1,)),
            pltpu.SemaphoreType.DMA((ng, 2)),
            pltpu.SemaphoreType.DMA((1,)),
            pltpu.SemaphoreType.DMA((2, 8)),
            pltpu.SemaphoreType.DMA((1,)),
            pltpu.SemaphoreType.DMA((2, 4)),
            pltpu.SemaphoreType.DMA((ng,)),
        ],
        compiler_params=pltpu.CompilerParams(
            collective_id=0, has_side_effects=True, vmem_limit_bytes=50 * 1024 * 1024
        ),
    )(orbitals.reshape(own * 128, NZ), potential.reshape(128, NZ))


def shards(orbitals, potential):
    basis, factor = filter_all(orbitals, potential)
    return (basis.reshape(orbitals.shape), factor)


def solution(mesh):
    covered = mesh.shape["space"] == 16 and mesh.shape["band"] == 2
    return jax.shard_map(
        shards if covered else general_shards,
        mesh=mesh,
        in_specs=(P("band", "space", None, None, None), P("space", None, None, None)),
        out_specs=(P("band", "space", None, None, None), P()),
        check_vma=False,
    )
```

```python
import functools

import jax
import jax.numpy as jnp
from jax import lax
from jax.experimental import pallas as pl
from jax.experimental.pallas import tpu as pltpu
from jax.sharding import PartitionSpec as P

DEG = 4
LAG, LEAD = 2, 3
NB = 8
LATE0 = 1
LATE1 = 8
MESH = pl.DeviceIdType.MESH

coefficients = (-205.0 / 72.0, 8.0 / 5.0, -1.0 / 5.0, 8.0 / 315.0, -1.0 / 560.0)
centre_value = 9.25
half_range = 4.75
filter_scale = 1.0 / 32.0


def shifted(block, axis, distance):
    devices = range(lax.axis_size(axis))
    route = [(i - distance, i) for i in devices if i - distance in devices]
    return lax.ppermute(block, axis, route)


def padded_along(field_in, axis_dim, stride, tile_count, coordinate):
    extent = field_in.shape[axis_dim]
    if tile_count == 1:
        widths = [(0, 0)] * field_in.ndim
        widths[axis_dim] = (4, 4)
        return jnp.pad(field_in, widths)
    top_layers = lax.slice_in_dim(field_in, extent - 4, extent, axis=axis_dim)
    bottom_layers = lax.slice_in_dim(field_in, 0, 4, axis=axis_dim)
    received = []
    for direction, portion, retain in (
        (1, top_layers, coordinate > 0),
        (-1, bottom_layers, coordinate < tile_count - 1),
    ):
        arrived = shifted(portion, "space", direction * stride)
        received.append(jnp.where(retain, arrived, jnp.zeros_like(arrived)))
    return jnp.concatenate([received[0], field_in, received[1]], axis=axis_dim)


def hamiltonian(field_in, potential, layout):
    total = 3.0 * coefficients[0] * field_in
    for axis_dim, stride, tile_count, coordinate in layout:
        padded = padded_along(field_in, axis_dim, stride, tile_count, coordinate)
        extent = field_in.shape[axis_dim]
        for offset in range(1, 5):
            upper = lax.slice_in_dim(padded, 4 + offset, 4 + offset + extent, axis=axis_dim)
            lower = lax.slice_in_dim(padded, 4 - offset, 4 - offset + extent, axis=axis_dim)
            total = total + coefficients[offset] * (upper + lower)
    return -0.5 * total + potential * field_in


def orthonormalize(flat, reduce_gram, total_cells, rows, own_count):
    count_orbs = flat.shape[0]
    identity = jnp.eye(count_orbs, dtype=jnp.float32)
    current = flat
    lowers = []
    for round_index in range(2):
        partial_gram = jnp.tensordot(
            current, current, axes=(tuple(range(1, current.ndim)),) * 2,
            precision=lax.Precision.HIGHEST, preferred_element_type=jnp.float32,
        )
        gram = reduce_gram(partial_gram) / total_cells
        lower = jnp.linalg.cholesky(gram)
        inverse = jax.scipy.linalg.solve_triangular(lower, identity, lower=True)
        if round_index == 1:
            inverse = lax.dynamic_slice_in_dim(inverse, rows, own_count, axis=0)
        current = jnp.tensordot(
            inverse, current, axes=1, precision=lax.Precision.HIGHEST, preferred_element_type=jnp.float32
        )
        lowers.append(lower)
    factor = jnp.dot(
        lowers[0], lowers[1], precision=lax.Precision.HIGHEST, preferred_element_type=jnp.float32
    ).T
    return (current, factor)


def reduce_everywhere(partial_gram):
    total = partial_gram
    size = lax.axis_size("space")
    step = 1
    while step < size:
        route = [(i, i ^ step) for i in range(size)]
        total = total + lax.ppermute(total, "space", route)
        step *= 2
    return total


def general_shards(orbitals, potential):
    tile_index = lax.axis_index("space")
    layout = (
        (2, 16, lax.axis_size("space") // 16, tile_index // 16),
        (3, 4, 4, tile_index // 4 % 4),
        (4, 1, 4, tile_index % 4),
    )
    previous = orbitals
    current = (hamiltonian(orbitals, potential, layout) - centre_value * orbitals) / half_range
    for step_index in range(DEG - 1):
        following = (
            2.0 * (hamiltonian(current, potential, layout) - centre_value * current) / half_range
            - previous
        )
        previous, current = (current, following)
    filtered = current * filter_scale
    own_count = filtered.shape[0]
    everything = lax.all_gather(filtered, "band", axis=0, tiled=True)
    total_cells = everything[0].size * lax.axis_size("space")
    rows = lax.axis_index("band") * own_count
    ortho, factor = orthonormalize(everything, reduce_everywhere, total_cells, rows, own_count)
    return (ortho.reshape(filtered.shape), factor)


NY, NXM, NZ = 16, 4, 128
ROWS = 16
UP, DOWN, LEFT, RIGHT = 0, 1, 2, 3


def kernel(
    ng, x_hbm, pot_ref, out_ref, factor_ref, x_ref, f_ref, y0, y1, y2, y3, pack, from_left, from_right, weight,
    stencil, along, lower_ref, gram, spread, plane, column, send, recv, xsend, xrecv, psend, precv, csend, crecv, fetch,
):
    ys = (y0, y1, y2, y3)
    cells = 16 * 8 * NY * NZ
    t = lax.axis_index("space")
    band = lax.axis_index("band")
    ty, tz = t // 4, t % 4
    lane = lax.broadcasted_iota(jnp.int32, (8, NZ), 1)
    sub = lax.broadcasted_iota(jnp.int32, (8, NZ), 0)
    even = sub % 2 == 0
    zero = jnp.zeros((8, NZ), jnp.float32)
    seat = lane % 8
    wide_lane = lax.broadcasted_iota(jnp.int32, (16, NZ), 1) // 8
    wide_row = lax.broadcasted_iota(jnp.int32, (16, NZ), 0) // 8
    seats = [wide_lane == 2 * j + wide_row for j in range(ROWS // 2)]

    def dot(a, b):
        return jnp.dot(a, b, preferred_element_type=jnp.float32)

    def parts(a):
        high = a.astype(jnp.bfloat16)
        rest = a - high.astype(jnp.float32)
        middle = rest.astype(jnp.bfloat16)
        low = (rest - middle.astype(jnp.float32)).astype(jnp.bfloat16)
        return high, middle, low

    source = lax.broadcasted_iota(jnp.int32, (2 * NZ, NZ), 0)
    target = lax.broadcasted_iota(jnp.int32, (2 * NZ, NZ), 1)
    m = source % 8
    source = jnp.where(source < NZ, source, jnp.where(m < 4, m - 4, 124 + m))
    apart = jnp.abs(source - target)
    taps = jnp.zeros((2 * NZ, NZ), jnp.float32)
    for k in range(1, 5):
        taps = jnp.where(apart == k, float(round(5040 * coefficients[k])), taps)
    stencil[...] = taps.astype(jnp.bfloat16)

    sends = (ty > 0, ty < 3, tz > 0, tz < 3)
    gets = (ty < 3, ty > 0, tz < 3, tz > 0)
    offset = (-4, 4, -1, 1)

    def halo(d, s, g):
        if d == UP:
            src, dst = ys[s].at[g, pl.ds(4, 4)], ys[s].at[g, pl.ds(20, 4)]
        elif d == DOWN:
            src, dst = ys[s].at[g, pl.ds(16, 4)], ys[s].at[g, pl.ds(0, 4)]
        elif d == LEFT:
            src, dst = pack.at[s, g], from_right.at[s, g]
        else:
            src, dst = pack.at[s, g], from_left.at[s, g]
        return pltpu.make_async_remote_copy(
            src_ref=src, dst_ref=dst, send_sem=send.at[d], recv_sem=recv.at[d, s, g],
            device_id=(t + offset[d], band), device_id_type=MESH,
        )

    def exchange(g, half):
        part = f_ref.at[band * ng + g, pl.ds(8 * half, 8)]
        return pltpu.make_async_remote_copy(
            src_ref=part, dst_ref=part, send_sem=xsend.at[0], recv_sem=xrecv.at[g, half],
            device_id=(t, 1 - band), device_id_type=MESH,
        )

    def arrival(g, half):
        part = f_ref.at[(1 - band) * ng + g, pl.ds(8 * half, 8)]
        return pltpu.make_async_remote_copy(
            src_ref=part, dst_ref=part, send_sem=xsend.at[0], recv_sem=xrecv.at[g, half],
            device_id=(t, 1 - band), device_id_type=MESH,
        )

    def fetched(g):
        rows = pl.ds(g * 512, 512)
        return pltpu.make_async_copy(x_hbm.at[rows], x_ref.at[rows], fetch.at[g])

    for g in range(ng):
        fetched(g).start()

    def clear(step, _):
        for s in range(4):
            @pl.when(ty == 0)
            def _():
                ys[s][step, 0:4] = jnp.zeros((4, NXM, 8, NZ), jnp.float32)

            @pl.when(ty == 3)
            def _():
                ys[s][step, 20:24] = jnp.zeros((4, NXM, 8, NZ), jnp.float32)

            @pl.when(tz == 0)
            def _():
                from_left[s, step] = jnp.zeros((4, 8, NZ), jnp.float32)

            @pl.when(tz == 3)
            def _():
                from_right[s, step] = jnp.zeros((4, 8, NZ), jnp.float32)
        return 0

    seat_in_plane = band * 4 + tz

    def in_plane(step):
        other = (seat_in_plane + step) % 8
        return other, (4 * ty + other % 4, other // 4)

    def in_column(step):
        other = (ty + step) % 4
        return other, (4 * other + tz, band)

    barrier = pltpu.get_barrier_semaphore()
    for step in range(1, 8):
        pl.semaphore_signal(barrier, inc=1, device_id=in_plane(step)[1], device_id_type=MESH)
    for step in range(1, 4):
        pl.semaphore_signal(barrier, inc=1, device_id=in_column(step)[1], device_id_type=MESH)

    def weigh(y, _):
        for xm in range(NXM):
            low = pot_ref[pl.ds(xm * NY + y, 1), :]
            high = pot_ref[pl.ds((4 + xm) * NY + y, 1), :]
            both = jnp.where(even, jnp.broadcast_to(low, (8, NZ)), jnp.broadcast_to(high, (8, NZ)))
            weight[y, xm] = (2.0 / half_range) * (both - (1.5 * coefficients[0] + centre_value))
        return 0


    def start_halos(s, g):
        for d in range(4):
            @pl.when(sends[d])
            def _():
                halo(d, s, g).start()

    def pack_edges(s, g):
        for q in range(4):
            packed = zero
            for j in range(ROWS):
                moved = pltpu.roll(ys[s][g, 4 + 4 * q + j // 4, j % 4], (8 * j + 4) % NZ, 1)
                packed = jnp.where(lane // 8 == j, moved, packed)
            pack[s, g, q] = packed

    def along_z(s, g):
        total = None
        inside = parts(ys[s][g, pl.ds(4, NY)].reshape(NY * NXM * 8, NZ))
        edges = [parts(jnp.where(seat < 4, from_left[s, g, q], from_right[s, g, q])) for q in range(4)]
        for which in range(3):
            seated = [
                jnp.where(seats[j], jnp.concatenate([edges[q][which]] * 2, axis=0), jnp.bfloat16(0))
                for q in range(4) for j in range(ROWS // 2)
            ]
            both = jnp.concatenate([inside[which], jnp.concatenate(seated, axis=0)], axis=1)
            term = dot(both, stencil[...])
            total = term if total is None else total + term
        along[...] = total.reshape(NY, NXM, 8, NZ)

    def prepare(g):
        fetched(g).wait()

        def quad(q, _):
            for j in range(ROWS):
                y, xm = 4 * q + j // 4, j % 4
                y0[g, 4 + y, xm] = x_ref[pl.ds(g * 512 + xm * NY + y, 8, stride=64), :]
            return 0

        lax.fori_loop(0, 4, quad, 0)
        pack_edges(0, g)

    def unit(s, g):
        for d in (LEFT, RIGHT):
            @pl.when(gets[d])
            def _():
                halo(d, s, g).wait_recv()
        now = ys[s]
        scale = (1.0 if s == 0 else 2.0) / half_range * (filter_scale if s == 3 else 1.0)
        keep = filter_scale if s == 3 else 1.0
        ck = [None] + [-0.5 * scale * c for c in coefficients[1:]]
        along_z(s, g)

        def quad(i, _):
            q = (i + 1) % 4
            for turn_of, d in ((2, UP), (3, DOWN)):
                @pl.when((i == turn_of) & gets[d])
                def _():
                    halo(d, s, g).wait_recv()

            for yy in range(4):
                y = 4 * q + yy
                v = [now[g, 4 + y, xm] for xm in range(NXM)]
                upper = [jnp.where(even, pltpu.roll(a, 7, 0), 0.0) for a in v]
                lower = [jnp.where(even, 0.0, pltpu.roll(a, 1, 0)) for a in v]
                for xm in range(NXM):
                    acc = (-0.5 * scale / 5040.0) * along[y, xm]
                    for k in range(1, 5):
                        total = now[g, 4 + y - k, xm] + now[g, 4 + y + k, xm]
                        right = v[xm + k] if xm + k < 4 else upper[xm + k - 4]
                        left = v[xm - k] if xm >= k else lower[xm - k + 4]
                        acc = acc + ck[k] * (total + (right + left))
                    w = weight[y, xm]
                    if s == 0:
                        new = acc + 0.5 * w * v[xm]
                    elif s == 3:
                        new = acc + (keep * w) * v[xm] - keep * ys[s - 1][g, 4 + y, xm]
                    else:
                        new = acc + w * v[xm] - ys[s - 1][g, 4 + y, xm]
                    if s < 3:
                        ys[s + 1][g, 4 + y, xm] = new
                    else:
                        f_ref[band * ng + g, y, xm] = new
            if s < 3:
                for turn_of, d in ((2, DOWN), (3, UP)):
                    @pl.when((i == turn_of) & sends[d])
                    def _():
                        halo(d, s + 1, g).start()
            return 0

        lax.fori_loop(0, 4, quad, 0)
        if s < 3:
            pack_edges(s + 1, g)
            for d in (LEFT, RIGHT):
                @pl.when(sends[d])
                def _():
                    halo(d, s + 1, g).start()
        else:
            exchange(g, 1 - band).start()

    lead = LEAD
    prepare(0)
    pl.semaphore_wait(barrier, 10)
    start_halos(0, 0)
    for g in range(1, lead):
        prepare(g)
        start_halos(0, g)
    lax.fori_loop(0, NY, weigh, 0)
    lax.fori_loop(0, ng, clear, 0)

    def turn(step, _):
        for s in (3, 2, 1, 0):
            g = step - LAG * s
            @pl.when((g >= 0) & (g < ng))
            def _():
                unit(s, g)

        @pl.when(step + lead < ng)
        def _():
            prepare(step + lead)
            start_halos(0, step + lead)
        return 0

    lax.fori_loop(0, ng + 3 * LAG, turn, 0)

    def shares(g, _):
        arrival(g, band).wait_recv()
        return 0

    lax.fori_loop(0, ng, shares, 0)

    def start_late(first, last):
        @pl.when(band == 0)
        def _():
            for piece in range(first, last):
                part = f_ref.at[piece // 2, pl.ds(4 * (piece % 2), 4)]
                pltpu.make_async_remote_copy(
                    src_ref=part, dst_ref=part, send_sem=xsend.at[0], recv_sem=xrecv.at[piece // 2, 0],
                    device_id=(t, 1 - band), device_id_type=MESH,
                ).start()

    start_late(0, LATE0)

    nr = 16 * ng
    norb = nr // 2
    tiles = norb // 8
    even_lane = lane % 2 == 0

    def block(y, xm):
        return f_ref[:, y, xm].reshape(nr, NZ)

    def line(y):
        return jnp.concatenate([block(y, xm) for xm in range(NXM)], axis=1)

    def inner(a):
        high, middle, low = parts(a)

        def dot_t(x, y):
            return lax.dot_general(x, y, (((1,), (1,)), ((), ())), preferred_element_type=jnp.float32)

        by_high = dot_t(jnp.concatenate([high, middle, low], axis=0), high)
        even_part = by_high[0:nr] + dot_t(middle, middle)
        return even_part, by_high[nr : 2 * nr] + by_high[2 * nr : 3 * nr]

    def apply_left(matrix_parts, a):
        m0, m1, m2 = matrix_parts
        a0, a1, a2 = parts(a)
        rows = m0.shape[0]
        lead = dot(
            jnp.concatenate([jnp.concatenate([m0, m0], axis=1), jnp.concatenate([m1, m1], axis=1)], axis=0),
            jnp.concatenate([a0, a1], axis=0),
        )
        rest = dot(jnp.concatenate([m2, m0], axis=1), jnp.concatenate([a0, a2], axis=0))
        return lead[0:rows] + (lead[rows:] + rest)

    def added(total, more):
        return total[0] + more[0], total[1] + more[1]

    def none():
        return jnp.zeros((nr, nr), jnp.float32), jnp.zeros((nr, nr), jnp.float32)

    def whole(total):
        return total[0] + (total[1] + total[1].T)

    def reduce_all(which, partial, meanwhile=lambda: None):
        gram[...] = jnp.zeros((nr, NZ), jnp.float32)
        gram[:, 0:nr] = partial
        first_half = gram[pl.ds(0, norb, stride=2), :]
        second_half = gram[pl.ds(1, norb, stride=2), :]
        both = [
            (first_half[8 * i : 8 * i + 8] + pltpu.roll(second_half[8 * i : 8 * i + 8], NZ - 1, 1)) * (1.0 / cells)
            for i in range(tiles)
        ]
        for i in range(tiles // 2):
            packed = jnp.where(even_lane, both[i], pltpu.roll(both[i + tiles // 2], 1, 1))
            plane[which, seat_in_plane, pl.ds(8 * i, 8)] = packed

        def to_plane(step):
            other, device = in_plane(step)
            mine = plane.at[which, seat_in_plane]
            return pltpu.make_async_remote_copy(
                src_ref=mine, dst_ref=mine, send_sem=psend.at[0], recv_sem=precv.at[which],
                device_id=device, device_id_type=MESH,
            )

        def to_column(step):
            other, device = in_column(step)
            mine = column.at[which, ty]
            return pltpu.make_async_remote_copy(
                src_ref=mine, dst_ref=mine, send_sem=csend.at[0], recv_sem=crecv.at[which],
                device_id=device, device_id_type=MESH,
            )

        def arrived(buffer, count, sem):
            bytes_of = buffer.at[which, pl.ds(0, count)]
            pltpu.make_async_remote_copy(
                src_ref=bytes_of, dst_ref=bytes_of, send_sem=psend.at[0], recv_sem=sem.at[which],
                device_id=(t, 1 - band), device_id_type=MESH,
            ).wait_recv()

        for step in range(1, 8):
            to_plane(step).start()
        meanwhile()
        arrived(plane, 7, precv)
        start_late(LATE0 if which == 0 else LATE1, LATE1 if which == 0 else 2 * ng)
        for i in range(tiles // 2):
            column[which, ty, pl.ds(8 * i, 8)] = sum(plane[which, o, pl.ds(8 * i, 8)] for o in range(8))
        for step in range(1, 4):
            to_column(step).start()
        arrived(column, 3, crecv)
        full = [sum(column[which, o, pl.ds(8 * i, 8)] for o in range(4)) for i in range(tiles // 2)]
        return [jnp.where(even_lane, a, pltpu.roll(a, 1, 1)) for a in full] + [
            jnp.where(even_lane, pltpu.roll(a, NZ - 1, 1), a) for a in full
        ]

    def eliminate(a, b):
        a, b = list(a), list(b)
        pivots = [zero + 1.0 for _ in range(tiles)]

        def across(v, j):
            return jnp.broadcast_to(v[:, 2 * j : 2 * j + 1], (8, NZ))

        for j in range(0, norb, NB):
            at, r = j // 8, j % 8
            row = [jnp.broadcast_to(a[at][r + k : r + k + 1, :], (8, NZ)) for k in range(NB)]
            row_b = [jnp.broadcast_to(b[at][r + k : r + k + 1, :], (8, NZ)) for k in range(NB)]
            cell = {(k, l): across(row[k], j + l) for k in range(NB) for l in range(k + 1)}
            inverse = []
            for k in range(NB):
                inverse.append(1.0 / cell[k, k])
                for l in range(k + 1, NB):
                    ratio = cell[l, k] * inverse[k]
                    for n in range(k + 1, l + 1):
                        cell[l, n] = cell[l, n] - ratio * cell[n, k]
                    row[l] = row[l] - ratio * row[k]
                    row_b[l] = row_b[l] - ratio * row_b[k]
            for i in range(at, tiles):
                if i == at and r + NB == 8:
                    continue
                share = []
                for k in range(NB):
                    col = across(a[i], j + k)
                    for l in range(k):
                        col = col - share[l] * cell[k, l]
                    share.append(col * inverse[k])
                if i == at:
                    share = [jnp.where(sub >= r + NB, m, 0.0) for m in share]
                taken, taken_b = [m * p for m, p in zip(share, row)], [m * p for m, p in zip(share, row_b)]
                while len(taken) > 1:
                    taken = [p + q for p, q in zip(taken[::2], taken[1::2])]
                    taken_b = [p + q for p, q in zip(taken_b[::2], taken_b[1::2])]
                a[i] = a[i] - taken[0]
                b[i] = b[i] - taken_b[0]
            for k in range(NB):
                a[at] = jnp.where(sub == r + k, row[k], a[at])
                b[at] = jnp.where(sub == r + k, row_b[k], b[at])
                pivots[at] = jnp.where(sub == r + k, cell[k, k], pivots[at])
        scale = [lax.rsqrt(p) for p in pivots]
        upper = [jnp.where(lane // 2 >= sub + 8 * i, a[i] * scale[i], 0.0) for i in range(tiles)]
        return upper, [b[i] * scale[i] for i in range(tiles)]

    def spread_rows(a):
        whole = jnp.concatenate(a, axis=0)
        is_even = jnp.concatenate([even_lane] * tiles, axis=0)
        spread[pl.ds(0, norb, stride=2), :] = jnp.where(is_even, whole, 0.0)
        spread[pl.ds(1, norb, stride=2), :] = jnp.where(is_even, 0.0, whole)

    def highest(a, b):
        return jnp.dot(a, b, precision=lax.Precision.HIGHEST, preferred_element_type=jnp.float32)

    def add_first(i, total):
        return added(total, inner(line(8 * band + i)))


    pick = jnp.where(
        lax.broadcasted_iota(jnp.int32, (NZ, norb), 0) == 2 * lax.broadcasted_iota(jnp.int32, (NZ, norb), 1), 1.0, 0.0
    )

    def run_tail():
        g1 = whole(lax.fori_loop(0, 8, add_first, none(), unroll=4))
        gram1 = reduce_all(0, g1)
        unit_rows = [jnp.where((lane // 2 == sub + 8 * i), 1.0, 0.0) for i in range(tiles)]
        upper1, inverse1 = eliminate(gram1, unit_rows)
        spread_rows(inverse1)

        left = parts(spread[:, 0:nr])

        def add_second(i, total):
            return added(total, inner(apply_left(left, line(8 * band + i))))
        g2 = whole(lax.fori_loop(0, 8, add_second, none(), unroll=4))
        def first_factor():
            lower_ref[...] = highest(jnp.concatenate(upper1, axis=0), pick)

        gram2 = reduce_all(1, g2, first_factor)
        upper2, inverse2 = eliminate(gram2, inverse1)
        spread_rows(inverse2)
        own = nr // 2
        factor_ref[...] = highest(highest(jnp.concatenate(upper2, axis=0), pick), lower_ref[...])
        @pl.when(band == 0)
        def _():
            def rows(i, _):
                y = i
                fields = jnp.concatenate([f_ref[0:ng, y, xm].reshape(own, NZ) for xm in range(NXM)], axis=1)
                result = apply_left(parts(spread[0:own, 0:own]), fields)
                for xm in range(NXM):
                    out_ref[pl.ds(xm * NY + y, own, stride=64), :] = result[:, NZ * xm : NZ * xm + NZ]
                return 0

            lax.fori_loop(0, NY, rows, 0, unroll=4)

        @pl.when(band == 1)
        def _():
            def rows(i, _):
                result = apply_left(parts(spread[own:nr, 0:nr]), line(i))
                for xm in range(NXM):
                    out_ref[pl.ds(xm * NY + i, own, stride=64), :] = result[:, NZ * xm : NZ * xm + NZ]
                return 0

            def late(g, _):
                arrival(g, 0).wait_recv()
                return 0

            lax.fori_loop(NY // 2, NY, rows, 0, unroll=4)
            lax.fori_loop(0, ng, late, 0)
            lax.fori_loop(0, NY // 2, rows, 0, unroll=4)

    run_tail()
    for sem, whole_of in ((psend, plane.at[:, pl.ds(0, 7)]), (csend, column.at[:, pl.ds(0, 3)])):
        pltpu.make_async_remote_copy(
            src_ref=whole_of, dst_ref=whole_of, send_sem=sem.at[0], recv_sem=precv.at[0],
            device_id=(t, 1 - band), device_id_type=MESH,
        ).wait_send()
    for d in range(4):
        everything = y0.at[:, pl.ds(0, 16)] if d < 2 else pack
        @pl.when(sends[d])
        def _():
            pltpu.make_async_remote_copy(
                src_ref=everything, dst_ref=everything, send_sem=send.at[d], recv_sem=recv.at[d, 0, 0],
                device_id=(t + offset[d], band), device_id_type=MESH,
            ).wait_send()

    def sent(whole):
        pltpu.make_async_remote_copy(
            src_ref=whole, dst_ref=whole, send_sem=xsend.at[0], recv_sem=xrecv.at[0, 0],
            device_id=(t, 1 - band), device_id_type=MESH,
        ).wait_send()

    @pl.when(band == 0)
    def _():
        sent(f_ref.at[pl.ds(0, ng)])

    @pl.when(band == 1)
    def _():
        sent(f_ref.at[pl.ds(0, ng), pl.ds(0, 8)])


def filter_all(orbitals, potential):
    own = orbitals.shape[0]
    ng = own // 4
    field = pltpu.VMEM((ng, NY + 8, NXM, 8, NZ), jnp.float32)
    edges = pltpu.VMEM((4, ng, 4, 8, NZ), jnp.float32)
    return pl.pallas_call(
        functools.partial(kernel, ng),
        out_shape=(
            jax.ShapeDtypeStruct((own * 128, NZ), jnp.float32),
            jax.ShapeDtypeStruct((2 * own, 2 * own), jnp.float32),
        ),
        in_specs=[pl.BlockSpec(memory_space=pl.ANY), pl.BlockSpec(memory_space=pltpu.VMEM)],
        out_specs=[pl.BlockSpec(memory_space=pltpu.VMEM)] * 2,
        scratch_shapes=[
            pltpu.VMEM((own * 128, NZ), jnp.float32),
            pltpu.VMEM((2 * ng, NY, NXM, 8, NZ), jnp.float32),
            field, field, field, field, edges, edges, edges,
            pltpu.VMEM((NY, NXM, 8, NZ), jnp.float32),
            pltpu.VMEM((2 * NZ, NZ), jnp.bfloat16),
            pltpu.VMEM((NY, NXM, 8, NZ), jnp.float32),
            pltpu.VMEM((8 * ng, 8 * ng), jnp.float32),
            pltpu.VMEM((16 * ng, NZ), jnp.float32),
            pltpu.VMEM((16 * ng, NZ), jnp.float32),
            pltpu.VMEM((2, 8, 4 * ng, NZ), jnp.float32),
            pltpu.VMEM((2, 4, 4 * ng, NZ), jnp.float32),
            pltpu.SemaphoreType.DMA((4,)),
            pltpu.SemaphoreType.DMA((4, 4, ng)),
            pltpu.SemaphoreType.DMA((1,)),
            pltpu.SemaphoreType.DMA((ng, 2)),
            pltpu.SemaphoreType.DMA((1,)),
            pltpu.SemaphoreType.DMA((2,)),
            pltpu.SemaphoreType.DMA((1,)),
            pltpu.SemaphoreType.DMA((2,)),
            pltpu.SemaphoreType.DMA((ng,)),
        ],
        compiler_params=pltpu.CompilerParams(
            collective_id=0, has_side_effects=True, vmem_limit_bytes=51 * 1024 * 1024
        ),
    )(orbitals.reshape(own * 128, NZ), potential.reshape(128, NZ))


def shards(orbitals, potential):
    basis, factor = filter_all(orbitals, potential)
    return (basis.reshape(orbitals.shape), factor)


def solution(mesh):
    covered = mesh.shape["space"] == 16 and mesh.shape["band"] == 2
    return jax.shard_map(
        shards if covered else general_shards,
        mesh=mesh,
        in_specs=(P("band", "space", None, None, None), P("space", None, None, None)),
        out_specs=(P("band", "space", None, None, None), P()),
        check_vma=False,
    )
```

```python
import functools

import jax
import jax.numpy as jnp
from jax import lax
from jax.experimental import pallas as pl
from jax.experimental.pallas import tpu as pltpu
from jax.sharding import PartitionSpec as P

DEG = 4
LAG, LEAD = 2, 4
NB = 8
LATE0 = 1
LATE1 = 8
MESH = pl.DeviceIdType.MESH

coefficients = (-205.0 / 72.0, 8.0 / 5.0, -1.0 / 5.0, 8.0 / 315.0, -1.0 / 560.0)
centre_value = 9.25
half_range = 4.75
filter_scale = 1.0 / 32.0


def shifted(block, axis, distance):
    devices = range(lax.axis_size(axis))
    route = [(i - distance, i) for i in devices if i - distance in devices]
    return lax.ppermute(block, axis, route)


def padded_along(field_in, axis_dim, stride, tile_count, coordinate):
    extent = field_in.shape[axis_dim]
    if tile_count == 1:
        widths = [(0, 0)] * field_in.ndim
        widths[axis_dim] = (4, 4)
        return jnp.pad(field_in, widths)
    top_layers = lax.slice_in_dim(field_in, extent - 4, extent, axis=axis_dim)
    bottom_layers = lax.slice_in_dim(field_in, 0, 4, axis=axis_dim)
    received = []
    for direction, portion, retain in (
        (1, top_layers, coordinate > 0),
        (-1, bottom_layers, coordinate < tile_count - 1),
    ):
        arrived = shifted(portion, "space", direction * stride)
        received.append(jnp.where(retain, arrived, jnp.zeros_like(arrived)))
    return jnp.concatenate([received[0], field_in, received[1]], axis=axis_dim)


def hamiltonian(field_in, potential, layout):
    total = 3.0 * coefficients[0] * field_in
    for axis_dim, stride, tile_count, coordinate in layout:
        padded = padded_along(field_in, axis_dim, stride, tile_count, coordinate)
        extent = field_in.shape[axis_dim]
        for offset in range(1, 5):
            upper = lax.slice_in_dim(padded, 4 + offset, 4 + offset + extent, axis=axis_dim)
            lower = lax.slice_in_dim(padded, 4 - offset, 4 - offset + extent, axis=axis_dim)
            total = total + coefficients[offset] * (upper + lower)
    return -0.5 * total + potential * field_in


def orthonormalize(flat, reduce_gram, total_cells, rows, own_count):
    count_orbs = flat.shape[0]
    identity = jnp.eye(count_orbs, dtype=jnp.float32)
    current = flat
    lowers = []
    for round_index in range(2):
        partial_gram = jnp.tensordot(
            current, current, axes=(tuple(range(1, current.ndim)),) * 2,
            precision=lax.Precision.HIGHEST, preferred_element_type=jnp.float32,
        )
        gram = reduce_gram(partial_gram) / total_cells
        lower = jnp.linalg.cholesky(gram)
        inverse = jax.scipy.linalg.solve_triangular(lower, identity, lower=True)
        if round_index == 1:
            inverse = lax.dynamic_slice_in_dim(inverse, rows, own_count, axis=0)
        current = jnp.tensordot(
            inverse, current, axes=1, precision=lax.Precision.HIGHEST, preferred_element_type=jnp.float32
        )
        lowers.append(lower)
    factor = jnp.dot(
        lowers[0], lowers[1], precision=lax.Precision.HIGHEST, preferred_element_type=jnp.float32
    ).T
    return (current, factor)


def reduce_everywhere(partial_gram):
    total = partial_gram
    size = lax.axis_size("space")
    step = 1
    while step < size:
        route = [(i, i ^ step) for i in range(size)]
        total = total + lax.ppermute(total, "space", route)
        step *= 2
    return total


def general_shards(orbitals, potential):
    tile_index = lax.axis_index("space")
    layout = (
        (2, 16, lax.axis_size("space") // 16, tile_index // 16),
        (3, 4, 4, tile_index // 4 % 4),
        (4, 1, 4, tile_index % 4),
    )
    previous = orbitals
    current = (hamiltonian(orbitals, potential, layout) - centre_value * orbitals) / half_range
    for step_index in range(DEG - 1):
        following = (
            2.0 * (hamiltonian(current, potential, layout) - centre_value * current) / half_range
            - previous
        )
        previous, current = (current, following)
    filtered = current * filter_scale
    own_count = filtered.shape[0]
    everything = lax.all_gather(filtered, "band", axis=0, tiled=True)
    total_cells = everything[0].size * lax.axis_size("space")
    rows = lax.axis_index("band") * own_count
    ortho, factor = orthonormalize(everything, reduce_everywhere, total_cells, rows, own_count)
    return (ortho.reshape(filtered.shape), factor)


NY, NXM, NZ = 16, 4, 128
ROWS = 16
UP, DOWN, LEFT, RIGHT = 0, 1, 2, 3


def kernel(
    ng, x_hbm, pot_ref, out_ref, factor_ref, x_ref, f_ref, y0, y1, y2, y3, pack, from_left, from_right, weight,
    stencil, along, lower_ref, gram, spread, plane, column, send, recv, xsend, xrecv, psend, precv, csend, crecv, fetch,
):
    ys = (y0, y1, y2, y3)
    cells = 16 * 8 * NY * NZ
    t = lax.axis_index("space")
    band = lax.axis_index("band")
    ty, tz = t // 4, t % 4
    lane = lax.broadcasted_iota(jnp.int32, (8, NZ), 1)
    sub = lax.broadcasted_iota(jnp.int32, (8, NZ), 0)
    even = sub % 2 == 0
    zero = jnp.zeros((8, NZ), jnp.float32)
    seat = lane % 8
    wide_lane = lax.broadcasted_iota(jnp.int32, (16, NZ), 1) // 8
    wide_row = lax.broadcasted_iota(jnp.int32, (16, NZ), 0) // 8
    seats = [wide_lane == 2 * j + wide_row for j in range(ROWS // 2)]

    def dot(a, b):
        return jnp.dot(a, b, preferred_element_type=jnp.float32)

    def parts(a):
        high = a.astype(jnp.bfloat16)
        rest = a - high.astype(jnp.float32)
        middle = rest.astype(jnp.bfloat16)
        low = (rest - middle.astype(jnp.float32)).astype(jnp.bfloat16)
        return high, middle, low

    source = lax.broadcasted_iota(jnp.int32, (2 * NZ, NZ), 0)
    target = lax.broadcasted_iota(jnp.int32, (2 * NZ, NZ), 1)
    m = source % 8
    source = jnp.where(source < NZ, source, jnp.where(m < 4, m - 4, 124 + m))
    apart = jnp.abs(source - target)
    taps = jnp.zeros((2 * NZ, NZ), jnp.float32)
    for k in range(1, 5):
        taps = jnp.where(apart == k, float(round(5040 * coefficients[k])), taps)
    stencil[...] = taps.astype(jnp.bfloat16)

    sends = (ty > 0, ty < 3, tz > 0, tz < 3)
    gets = (ty < 3, ty > 0, tz < 3, tz > 0)
    offset = (-4, 4, -1, 1)

    def halo(d, s, g):
        if d == UP:
            src, dst = ys[s].at[g, pl.ds(4, 4)], ys[s].at[g, pl.ds(20, 4)]
        elif d == DOWN:
            src, dst = ys[s].at[g, pl.ds(16, 4)], ys[s].at[g, pl.ds(0, 4)]
        elif d == LEFT:
            src, dst = pack.at[s, g], from_right.at[s, g]
        else:
            src, dst = pack.at[s, g], from_left.at[s, g]
        return pltpu.make_async_remote_copy(
            src_ref=src, dst_ref=dst, send_sem=send.at[d], recv_sem=recv.at[d, s, g],
            device_id=(t + offset[d], band), device_id_type=MESH,
        )

    def exchange(g, half):
        part = f_ref.at[band * ng + g, pl.ds(8 * half, 8)]
        return pltpu.make_async_remote_copy(
            src_ref=part, dst_ref=part, send_sem=xsend.at[0], recv_sem=xrecv.at[g, half],
            device_id=(t, 1 - band), device_id_type=MESH,
        )

    def arrival(g, half):
        part = f_ref.at[(1 - band) * ng + g, pl.ds(8 * half, 8)]
        return pltpu.make_async_remote_copy(
            src_ref=part, dst_ref=part, send_sem=xsend.at[0], recv_sem=xrecv.at[g, half],
            device_id=(t, 1 - band), device_id_type=MESH,
        )

    def fetched(g):
        rows = pl.ds(g * 512, 512)
        return pltpu.make_async_copy(x_hbm.at[rows], x_ref.at[rows], fetch.at[g])

    for g in range(ng):
        fetched(g).start()

    def clear(step, _):
        for s in range(4):
            @pl.when(ty == 0)
            def _():
                ys[s][step, 0:4] = jnp.zeros((4, NXM, 8, NZ), jnp.float32)

            @pl.when(ty == 3)
            def _():
                ys[s][step, 20:24] = jnp.zeros((4, NXM, 8, NZ), jnp.float32)

            @pl.when(tz == 0)
            def _():
                from_left[s, step] = jnp.zeros((4, 8, NZ), jnp.float32)

            @pl.when(tz == 3)
            def _():
                from_right[s, step] = jnp.zeros((4, 8, NZ), jnp.float32)
        return 0

    seat_in_plane = band * 4 + tz

    def in_plane(step):
        other = (seat_in_plane + step) % 8
        return other, (4 * ty + other % 4, other // 4)

    def in_column(step):
        other = (ty + step) % 4
        return other, (4 * other + tz, band)

    barrier = pltpu.get_barrier_semaphore()
    for step in range(1, 8):
        pl.semaphore_signal(barrier, inc=1, device_id=in_plane(step)[1], device_id_type=MESH)
    for step in range(1, 4):
        pl.semaphore_signal(barrier, inc=1, device_id=in_column(step)[1], device_id_type=MESH)

    def weigh(y, _):
        for xm in range(NXM):
            low = pot_ref[pl.ds(xm * NY + y, 1), :]
            high = pot_ref[pl.ds((4 + xm) * NY + y, 1), :]
            both = jnp.where(even, jnp.broadcast_to(low, (8, NZ)), jnp.broadcast_to(high, (8, NZ)))
            weight[y, xm] = (2.0 / half_range) * (both - (1.5 * coefficients[0] + centre_value))
        return 0


    def start_halos(s, g):
        for d in range(4):
            @pl.when(sends[d])
            def _():
                halo(d, s, g).start()

    def pack_edges(s, g):
        for q in range(4):
            packed = zero
            for j in range(ROWS):
                moved = pltpu.roll(ys[s][g, 4 + 4 * q + j // 4, j % 4], (8 * j + 4) % NZ, 1)
                packed = jnp.where(lane // 8 == j, moved, packed)
            pack[s, g, q] = packed

    def along_z(s, g):
        total = None
        inside = parts(ys[s][g, pl.ds(4, NY)].reshape(NY * NXM * 8, NZ))
        edges = [parts(jnp.where(seat < 4, from_left[s, g, q], from_right[s, g, q])) for q in range(4)]
        for which in range(3):
            seated = [
                jnp.where(seats[j], jnp.concatenate([edges[q][which]] * 2, axis=0), jnp.bfloat16(0))
                for q in range(4) for j in range(ROWS // 2)
            ]
            both = jnp.concatenate([inside[which], jnp.concatenate(seated, axis=0)], axis=1)
            term = dot(both, stencil[...])
            total = term if total is None else total + term
        along[...] = total.reshape(NY, NXM, 8, NZ)

    def prepare(g):
        fetched(g).wait()

        def quad(q, _):
            for j in range(ROWS):
                y, xm = 4 * q + j // 4, j % 4
                y0[g, 4 + y, xm] = x_ref[pl.ds(g * 512 + xm * NY + y, 8, stride=64), :]
            return 0

        lax.fori_loop(0, 4, quad, 0)
        pack_edges(0, g)

    def unit(s, g):
        for d in (LEFT, RIGHT):
            @pl.when(gets[d])
            def _():
                halo(d, s, g).wait_recv()
        now = ys[s]
        scale = (1.0 if s == 0 else 2.0) / half_range * (filter_scale if s == 3 else 1.0)
        keep = filter_scale if s == 3 else 1.0
        ck = [None] + [-0.5 * scale * c for c in coefficients[1:]]
        along_z(s, g)

        def quad(i, _):
            q = (i + 1) % 4
            for turn_of, d in ((2, UP), (3, DOWN)):
                @pl.when((i == turn_of) & gets[d])
                def _():
                    halo(d, s, g).wait_recv()

            for yy in range(4):
                y = 4 * q + yy
                v = [now[g, 4 + y, xm] for xm in range(NXM)]
                upper = [jnp.where(even, pltpu.roll(a, 7, 0), 0.0) for a in v]
                lower = [jnp.where(even, 0.0, pltpu.roll(a, 1, 0)) for a in v]
                for xm in range(NXM):
                    acc = (-0.5 * scale / 5040.0) * along[y, xm]
                    for k in range(1, 5):
                        total = now[g, 4 + y - k, xm] + now[g, 4 + y + k, xm]
                        right = v[xm + k] if xm + k < 4 else upper[xm + k - 4]
                        left = v[xm - k] if xm >= k else lower[xm - k + 4]
                        acc = acc + ck[k] * (total + (right + left))
                    w = weight[y, xm]
                    if s == 0:
                        new = acc + 0.5 * w * v[xm]
                    elif s == 3:
                        new = acc + (keep * w) * v[xm] - keep * ys[s - 1][g, 4 + y, xm]
                    else:
                        new = acc + w * v[xm] - ys[s - 1][g, 4 + y, xm]
                    if s < 3:
                        ys[s + 1][g, 4 + y, xm] = new
                    else:
                        f_ref[band * ng + g, y, xm] = new
            if s < 3:
                for turn_of, d in ((2, DOWN), (3, UP)):
                    @pl.when((i == turn_of) & sends[d])
                    def _():
                        halo(d, s + 1, g).start()
            return 0

        lax.fori_loop(0, 4, quad, 0)
        if s < 3:
            pack_edges(s + 1, g)
            for d in (LEFT, RIGHT):
                @pl.when(sends[d])
                def _():
                    halo(d, s + 1, g).start()
        else:
            exchange(g, 1 - band).start()

    lead = LEAD
    prepare(0)
    pl.semaphore_wait(barrier, 10)
    start_halos(0, 0)
    for g in range(1, lead):
        prepare(g)
        start_halos(0, g)
    lax.fori_loop(0, NY, weigh, 0)
    lax.fori_loop(0, ng, clear, 0)

    def turn(step, _):
        for s in (3, 2, 1, 0):
            g = step - LAG * s
            @pl.when((g >= 0) & (g < ng))
            def _():
                unit(s, g)

        @pl.when(step + lead < ng)
        def _():
            prepare(step + lead)
            start_halos(0, step + lead)
        return 0

    lax.fori_loop(0, ng + 3 * LAG, turn, 0)

    def shares(g, _):
        arrival(g, band).wait_recv()
        return 0

    lax.fori_loop(0, ng, shares, 0)

    def start_late(first, last):
        @pl.when(band == 0)
        def _():
            for piece in range(first, last):
                part = f_ref.at[piece // 2, pl.ds(4 * (piece % 2), 4)]
                pltpu.make_async_remote_copy(
                    src_ref=part, dst_ref=part, send_sem=xsend.at[0], recv_sem=xrecv.at[piece // 2, 0],
                    device_id=(t, 1 - band), device_id_type=MESH,
                ).start()

    start_late(0, LATE0)

    nr = 16 * ng
    norb = nr // 2
    tiles = norb // 8
    even_lane = lane % 2 == 0

    def block(y, xm):
        return f_ref[:, y, xm].reshape(nr, NZ)

    def line(y):
        return jnp.concatenate([block(y, xm) for xm in range(NXM)], axis=1)

    def inner(a):
        high, middle, low = parts(a)

        def dot_t(x, y):
            return lax.dot_general(x, y, (((1,), (1,)), ((), ())), preferred_element_type=jnp.float32)

        by_high = dot_t(jnp.concatenate([high, middle, low], axis=0), high)
        even_part = by_high[0:nr] + dot_t(middle, middle)
        return even_part, by_high[nr : 2 * nr] + by_high[2 * nr : 3 * nr]

    def apply_left(matrix_parts, a):
        m0, m1, m2 = matrix_parts
        a0, a1, a2 = parts(a)
        rows = m0.shape[0]
        lead = dot(
            jnp.concatenate([jnp.concatenate([m0, m0], axis=1), jnp.concatenate([m1, m1], axis=1)], axis=0),
            jnp.concatenate([a0, a1], axis=0),
        )
        rest = dot(jnp.concatenate([m2, m0], axis=1), jnp.concatenate([a0, a2], axis=0))
        return lead[0:rows] + (lead[rows:] + rest)

    def added(total, more):
        return total[0] + more[0], total[1] + more[1]

    def none():
        return jnp.zeros((nr, nr), jnp.float32), jnp.zeros((nr, nr), jnp.float32)

    def whole(total):
        return total[0] + (total[1] + total[1].T)

    def reduce_all(which, partial, meanwhile=lambda: None):
        gram[...] = jnp.zeros((nr, NZ), jnp.float32)
        gram[:, 0:nr] = partial
        first_half = gram[pl.ds(0, norb, stride=2), :]
        second_half = gram[pl.ds(1, norb, stride=2), :]
        both = [
            (first_half[8 * i : 8 * i + 8] + pltpu.roll(second_half[8 * i : 8 * i + 8], NZ - 1, 1)) * (1.0 / cells)
            for i in range(tiles)
        ]
        for i in range(tiles // 2):
            packed = jnp.where(even_lane, both[i], pltpu.roll(both[i + tiles // 2], 1, 1))
            plane[which, seat_in_plane, pl.ds(8 * i, 8)] = packed

        def to_plane(step):
            other, device = in_plane(step)
            mine = plane.at[which, seat_in_plane]
            return pltpu.make_async_remote_copy(
                src_ref=mine, dst_ref=mine, send_sem=psend.at[0], recv_sem=precv.at[which],
                device_id=device, device_id_type=MESH,
            )

        def to_column(step):
            other, device = in_column(step)
            mine = column.at[which, ty]
            return pltpu.make_async_remote_copy(
                src_ref=mine, dst_ref=mine, send_sem=csend.at[0], recv_sem=crecv.at[which],
                device_id=device, device_id_type=MESH,
            )

        def arrived(buffer, count, sem):
            bytes_of = buffer.at[which, pl.ds(0, count)]
            pltpu.make_async_remote_copy(
                src_ref=bytes_of, dst_ref=bytes_of, send_sem=psend.at[0], recv_sem=sem.at[which],
                device_id=(t, 1 - band), device_id_type=MESH,
            ).wait_recv()

        for step in (6, 2, 5, 3, 4, 7, 1):
            to_plane(step).start()
        meanwhile()
        arrived(plane, 7, precv)
        start_late(LATE0 if which == 0 else LATE1, LATE1 if which == 0 else 2 * ng)
        for i in range(tiles // 2):
            column[which, ty, pl.ds(8 * i, 8)] = sum(plane[which, o, pl.ds(8 * i, 8)] for o in range(8))
        for step in range(1, 4):
            to_column(jnp.where(ty < 2, 4 - step, step)).start()
        arrived(column, 3, crecv)
        full = [sum(column[which, o, pl.ds(8 * i, 8)] for o in range(4)) for i in range(tiles // 2)]
        return [jnp.where(even_lane, a, pltpu.roll(a, 1, 1)) for a in full] + [
            jnp.where(even_lane, pltpu.roll(a, NZ - 1, 1), a) for a in full
        ]

    def eliminate(a, b):
        a, b = list(a), list(b)
        pivots = [zero + 1.0 for _ in range(tiles)]

        def across(v, j):
            return jnp.broadcast_to(v[:, 2 * j : 2 * j + 1], (8, NZ))

        for j in range(0, norb, NB):
            at, r = j // 8, j % 8
            row = [jnp.broadcast_to(a[at][r + k : r + k + 1, :], (8, NZ)) for k in range(NB)]
            row_b = [jnp.broadcast_to(b[at][r + k : r + k + 1, :], (8, NZ)) for k in range(NB)]
            cell = {(k, l): across(row[k], j + l) for k in range(NB) for l in range(k + 1)}
            inverse = []
            for k in range(NB):
                inverse.append(1.0 / cell[k, k])
                for l in range(k + 1, NB):
                    ratio = cell[l, k] * inverse[k]
                    for n in range(k + 1, l + 1):
                        cell[l, n] = cell[l, n] - ratio * cell[n, k]
                    row[l] = row[l] - ratio * row[k]
                    row_b[l] = row_b[l] - ratio * row_b[k]
            for i in range(at, tiles):
                if i == at and r + NB == 8:
                    continue
                share = []
                for k in range(NB):
                    col = across(a[i], j + k)
                    for l in range(k):
                        col = col - share[l] * cell[k, l]
                    share.append(col * inverse[k])
                if i == at:
                    share = [jnp.where(sub >= r + NB, m, 0.0) for m in share]
                taken, taken_b = [m * p for m, p in zip(share, row)], [m * p for m, p in zip(share, row_b)]
                while len(taken) > 1:
                    taken = [p + q for p, q in zip(taken[::2], taken[1::2])]
                    taken_b = [p + q for p, q in zip(taken_b[::2], taken_b[1::2])]
                a[i] = a[i] - taken[0]
                b[i] = b[i] - taken_b[0]
            for k in range(NB):
                a[at] = jnp.where(sub == r + k, row[k], a[at])
                b[at] = jnp.where(sub == r + k, row_b[k], b[at])
                pivots[at] = jnp.where(sub == r + k, cell[k, k], pivots[at])
        scale = [lax.rsqrt(p) for p in pivots]
        upper = [jnp.where(lane // 2 >= sub + 8 * i, a[i] * scale[i], 0.0) for i in range(tiles)]
        return upper, [b[i] * scale[i] for i in range(tiles)]

    def spread_rows(a):
        whole = jnp.concatenate(a, axis=0)
        is_even = jnp.concatenate([even_lane] * tiles, axis=0)
        spread[pl.ds(0, norb, stride=2), :] = jnp.where(is_even, whole, 0.0)
        spread[pl.ds(1, norb, stride=2), :] = jnp.where(is_even, 0.0, whole)

    def highest(a, b):
        return jnp.dot(a, b, precision=lax.Precision.HIGHEST, preferred_element_type=jnp.float32)

    def add_first(i, total):
        return added(total, inner(line(8 * band + i)))


    pick = jnp.where(
        lax.broadcasted_iota(jnp.int32, (NZ, norb), 0) == 2 * lax.broadcasted_iota(jnp.int32, (NZ, norb), 1), 1.0, 0.0
    )

    def run_tail():
        g1 = whole(lax.fori_loop(0, 8, add_first, none(), unroll=4))
        gram1 = reduce_all(0, g1)
        unit_rows = [jnp.where((lane // 2 == sub + 8 * i), 1.0, 0.0) for i in range(tiles)]
        upper1, inverse1 = eliminate(gram1, unit_rows)
        spread_rows(inverse1)

        left = parts(spread[:, 0:nr])

        def add_second(i, total):
            return added(total, inner(apply_left(left, line(8 * band + i))))
        g2 = whole(lax.fori_loop(0, 8, add_second, none(), unroll=4))
        def first_factor():
            lower_ref[...] = highest(jnp.concatenate(upper1, axis=0), pick)

        gram2 = reduce_all(1, g2, first_factor)
        upper2, inverse2 = eliminate(gram2, inverse1)
        spread_rows(inverse2)
        own = nr // 2
        factor_ref[...] = highest(highest(jnp.concatenate(upper2, axis=0), pick), lower_ref[...])
        @pl.when(band == 0)
        def _():
            def rows(i, _):
                y = i
                fields = jnp.concatenate([f_ref[0:ng, y, xm].reshape(own, NZ) for xm in range(NXM)], axis=1)
                result = apply_left(parts(spread[0:own, 0:own]), fields)
                for xm in range(NXM):
                    out_ref[pl.ds(xm * NY + y, own, stride=64), :] = result[:, NZ * xm : NZ * xm + NZ]
                return 0

            lax.fori_loop(0, NY, rows, 0, unroll=8)

        @pl.when(band == 1)
        def _():
            def rows(i, _):
                result = apply_left(parts(spread[own:nr, 0:nr]), line(i))
                for xm in range(NXM):
                    out_ref[pl.ds(xm * NY + i, own, stride=64), :] = result[:, NZ * xm : NZ * xm + NZ]
                return 0

            def late(g, _):
                arrival(g, 0).wait_recv()
                return 0

            lax.fori_loop(NY // 2, NY, rows, 0, unroll=8)
            lax.fori_loop(0, ng, late, 0)
            lax.fori_loop(0, NY // 2, rows, 0, unroll=8)

    run_tail()
    for sem, whole_of in ((psend, plane.at[:, pl.ds(0, 7)]), (csend, column.at[:, pl.ds(0, 3)])):
        pltpu.make_async_remote_copy(
            src_ref=whole_of, dst_ref=whole_of, send_sem=sem.at[0], recv_sem=precv.at[0],
            device_id=(t, 1 - band), device_id_type=MESH,
        ).wait_send()
    for d in range(4):
        everything = y0.at[:, pl.ds(0, 16)] if d < 2 else pack
        @pl.when(sends[d])
        def _():
            pltpu.make_async_remote_copy(
                src_ref=everything, dst_ref=everything, send_sem=send.at[d], recv_sem=recv.at[d, 0, 0],
                device_id=(t + offset[d], band), device_id_type=MESH,
            ).wait_send()

    def sent(whole):
        pltpu.make_async_remote_copy(
            src_ref=whole, dst_ref=whole, send_sem=xsend.at[0], recv_sem=xrecv.at[0, 0],
            device_id=(t, 1 - band), device_id_type=MESH,
        ).wait_send()

    @pl.when(band == 0)
    def _():
        sent(f_ref.at[pl.ds(0, ng)])

    @pl.when(band == 1)
    def _():
        sent(f_ref.at[pl.ds(0, ng), pl.ds(0, 8)])


def filter_all(orbitals, potential):
    own = orbitals.shape[0]
    ng = own // 4
    field = pltpu.VMEM((ng, NY + 8, NXM, 8, NZ), jnp.float32)
    edges = pltpu.VMEM((4, ng, 4, 8, NZ), jnp.float32)
    return pl.pallas_call(
        functools.partial(kernel, ng),
        out_shape=(
            jax.ShapeDtypeStruct((own * 128, NZ), jnp.float32),
            jax.ShapeDtypeStruct((2 * own, 2 * own), jnp.float32),
        ),
        in_specs=[pl.BlockSpec(memory_space=pl.ANY), pl.BlockSpec(memory_space=pltpu.VMEM)],
        out_specs=[pl.BlockSpec(memory_space=pltpu.VMEM)] * 2,
        scratch_shapes=[
            pltpu.VMEM((own * 128, NZ), jnp.float32),
            pltpu.VMEM((2 * ng, NY, NXM, 8, NZ), jnp.float32),
            field, field, field, field, edges, edges, edges,
            pltpu.VMEM((NY, NXM, 8, NZ), jnp.float32),
            pltpu.VMEM((2 * NZ, NZ), jnp.bfloat16),
            pltpu.VMEM((NY, NXM, 8, NZ), jnp.float32),
            pltpu.VMEM((8 * ng, 8 * ng), jnp.float32),
            pltpu.VMEM((16 * ng, NZ), jnp.float32),
            pltpu.VMEM((16 * ng, NZ), jnp.float32),
            pltpu.VMEM((2, 8, 4 * ng, NZ), jnp.float32),
            pltpu.VMEM((2, 4, 4 * ng, NZ), jnp.float32),
            pltpu.SemaphoreType.DMA((4,)),
            pltpu.SemaphoreType.DMA((4, 4, ng)),
            pltpu.SemaphoreType.DMA((1,)),
            pltpu.SemaphoreType.DMA((ng, 2)),
            pltpu.SemaphoreType.DMA((1,)),
            pltpu.SemaphoreType.DMA((2,)),
            pltpu.SemaphoreType.DMA((1,)),
            pltpu.SemaphoreType.DMA((2,)),
            pltpu.SemaphoreType.DMA((ng,)),
        ],
        compiler_params=pltpu.CompilerParams(
            collective_id=0, has_side_effects=True, vmem_limit_bytes=51 * 1024 * 1024
        ),
    )(orbitals.reshape(own * 128, NZ), potential.reshape(128, NZ))


def shards(orbitals, potential):
    basis, factor = filter_all(orbitals, potential)
    return (basis.reshape(orbitals.shape), factor)


def solution(mesh):
    covered = mesh.shape["space"] == 16 and mesh.shape["band"] == 2
    return jax.shard_map(
        shards if covered else general_shards,
        mesh=mesh,
        in_specs=(P("band", "space", None, None, None), P("space", None, None, None)),
        out_specs=(P("band", "space", None, None, None), P()),
        check_vma=False,
    )
```
